128 devices in a mesh: occ: 32 (over x, z, core), rep: 4 (over y).
Axes of the slice: x: 4, y: 4, z: 4, core: 2. Of those that a mesh axis runs over, the one named last changes fastest.
Arguments:
- coeffs: bfloat16 [512, 12, 64, 128], P(('occ', 'rep')), may hold values from -1 to 1
- amplitudes: bfloat16 [512, 4096], P(('occ', 'rep')), may hold values from -6 to 6
- denominators: float32 [512, 64], P(('occ', 'rep')), may hold values from 0.25 to 2
- pno_count: int32 [512], P(('occ', 'rep')), may hold values from 24 to 64
- domains: int32 [512, 12], replicated, may hold values from 0 to 31, as said below
- far_owner: int32 [512, 2], P(('occ', 'rep')), may hold values from 0 to 31, all different within a row; in each aligned block of 4 rows (0 to 3, 4 to 7, ...) at most 2 rows name the same one
- far_pair: int32 [512, 2], P(('occ', 'rep')), may hold values from 0 to 3
- near_pair: int32 [512, 40], P(('occ', 'rep')), may hold values from 0 to 15
Outputs:
- residual: float32 [512, 4096], P(('occ', 'rep'))
The draws below stay inside these ranges and needn't reach their ends.
Inputs may be any that keep to these rules, and one draw needn't show every extreme that they name: `domains`: each row names 12 different blocks. `far_owner`: the 2 entries of a row differ; among the rows of one device no occupied block is named more than 2 times, and that bound is reached.
All inputs are finite; a program needn't handle non-finite values.
Results may differ from the reference program's by a relative error of at most 0.0003.
Values may be sent and summed in bfloat16 or wider, within the bound.
A program may use at most 128 MiB of HBM per device.

```python
import math
import jax
import jax.numpy as jnp
import numpy as np
from jax import lax

NPNO = 64
BLK = 128
DOMB = 12
NBLK = 32
KN = 2
KL = 40
P_DEV = 4
NP = 512
CAP = 2
N_OCC = 32
N_REP = 4


def draw_domains(key, part):
    row_keys = jax.random.split(jax.random.fold_in(key, 7), NP)
    picked = jax.vmap(lambda row_key: jax.random.permutation(row_key, NBLK)[:DOMB])(row_keys)
    return picked.astype(jnp.int32)


def place_ends(entries, key, smallest, top_value):
    shape = entries.shape
    index_at = [jax.random.randint(jax.random.fold_in(key, axis), (), 0, shape[axis]) for axis in range(len(shape))]
    entries = entries.at[tuple(index_at)].set(smallest)
    longest = shape.index(max(shape))
    index_at[longest] = (index_at[longest] + 1) % shape[longest]
    return entries.at[tuple(index_at)].set(top_value)


def block_levels(own_key, extent, shards, low, largest):
    factor_of = 1.0
    for axis_at, shards_of in shards:
        steps = jax.random.uniform(jax.random.fold_in(jax.random.fold_in(own_key, 6), axis_at), (shards_of,), jnp.float32, low / len(shards), largest / len(shards))
        factor_of = factor_of * jnp.repeat(jnp.exp(steps), extent[axis_at] // shards_of).reshape((-1,) + (1,) * (len(extent) - 1 - axis_at))
    return factor_of


def deal_out(own_key, own, number, rows, count, top, most, skew):
    sequence = jax.random.permutation(own_key, count)
    packed, common = shares(count, rows * top, most, skew, True), shares(count, rows * top, most, skew, False)
    places = jnp.arange(count)

    def named(lengths, rotation):
        used = int((lengths > 0).sum())
        fixed = max(1, used // 4)
        shifted = fixed + (places - fixed + rotation * (used - fixed)) % max(1, count - fixed)
        return jnp.zeros((count,), jnp.int32).at[sequence[jnp.where(places < fixed, places, shifted)]].set(jnp.asarray(lengths, jnp.int32))

    lengths = jnp.where(number % 4 == 0, named(packed, number // 4), named(common, number - number // 4 - 1))
    mixed = jax.random.permutation(jax.random.fold_in(own, 3), count)
    source_of, sink = mixed[0:count // 2 * 2:2], mixed[1:count // 2 * 2:2]
    slack = jnp.minimum(lengths[source_of] - 1, most - lengths[sink]) // 2
    slack = jnp.where((source_of == sequence[0]) | (sink == sequence[0]) | (lengths[sink] == 0), 0, jnp.maximum(slack, 0))
    shifted = jax.random.randint(jax.random.fold_in(own, 4), (count // 2,), 0, 1 << 20) % (slack + 1)
    lengths = lengths.at[source_of].add(-shifted).at[sink].add(shifted)
    members = jnp.searchsorted(jnp.cumsum(lengths), jnp.arange(rows * top), side="right").astype(jnp.int32)
    grid = members.reshape(top, rows).T
    grid = grid[jax.random.permutation(jax.random.fold_in(own, 1), rows)]
    rotation = jax.random.randint(jax.random.fold_in(own, 2), (rows, 1), 0, top)
    return jnp.take_along_axis(grid, (jnp.arange(top)[None, :] + rotation) % top, axis=1)


def shares(amount, total, limit, skew, full):
    weights = [(1 << 20) // math.isqrt(standing ** skew) + 1 for standing in range(1, amount + 1)]
    largest = limit if full else min(limit, max(-(-total // amount), total * weights[0] // sum(weights)))
    least = 1 if total - largest >= amount - 1 else 0
    holding, surplus = [largest] + [least] * (amount - 1), total - largest - least * (amount - 1)
    while surplus > 0:
        free = [i for i in range(1, amount) if holding[i] < largest] or [i for i in range(1, amount) if holding[i] < limit]
        whole, remaining = sum([weights[i] for i in free]), surplus
        for i in free:
            extra = min(limit - holding[i], max(1, remaining * weights[i] // whole), surplus)
            holding[i] = holding[i] + extra
            surplus = surplus - extra
    return np.array(holding)


def gaussian(key, extent, spread, most, shards=(), held_as=jnp.bfloat16):
    values = spread * jax.random.normal(key, extent, jnp.float32)
    if shards:
        values = values * block_levels(key, extent, shards, -0.22, 0.18)
    return jnp.clip(values, -most, most).astype(held_as)


def setup_inputs(seed: int = 0) -> dict:
    seeds = jax.random.split(jax.random.key(seed), 9)
    coeffs = gaussian(seeds[0], (NP, DOMB, NPNO, BLK), ((NPNO * DOMB * DOMB * BLK / NBLK) ** -0.25), 1.0, ((0, 128),))
    amplitudes = gaussian(seeds[1], (NP, NPNO * NPNO), 1.0, 6.0, ((0, 128),))
    denominators = jnp.clip(jnp.exp(math.log(2.0) - 2.0794415 * jax.random.uniform(seeds[2], (NP, NPNO), jnp.float32) ** block_levels(seeds[2], (NP, NPNO), ((0, 128),), -0.2, 0.2)), 0.25, 2.0)
    pno_count = place_ends(jax.random.randint(seeds[3], (NP,), 3 * NPNO // 8, NPNO + 1), jax.random.fold_in(seeds[3], 1), 3 * NPNO // 8, NPNO).astype(jnp.int32)
    domains = draw_domains(jax.random.fold_in(seeds[8], 71), 0)
    far_owner_keys = jax.random.split(jax.random.fold_in(seeds[5], 1), NP // P_DEV)
    far_owner_turns = jax.random.permutation(jax.random.fold_in(seeds[5], 3), NP // P_DEV)
    far_owner = jax.vmap(lambda own, number: deal_out(jax.random.fold_in(seeds[5], 2), own, number, P_DEV, N_OCC, KN, CAP, 2))(far_owner_keys, far_owner_turns).reshape((NP, KN))
    far_pair = place_ends(jax.random.randint(seeds[6], (NP, KN), 0, P_DEV), jax.random.fold_in(seeds[6], 1), 0, P_DEV - 1).astype(jnp.int32)
    near_pair = place_ends(jax.random.randint(seeds[7], (NP, KL), 0, N_REP * P_DEV), jax.random.fold_in(seeds[7], 1), 0, (N_REP * P_DEV) - 1).astype(jnp.int32)
    return dict(coeffs=coeffs, amplitudes=amplitudes, denominators=denominators, pno_count=pno_count, domains=domains, far_owner=far_owner, far_pair=far_pair, near_pair=near_pair)


def intersection(left_coeff, left_dom, right_coeff, right_dom):
    matches = (left_dom[:, None] == right_dom[None, :]).astype(jnp.float32)
    flat = right_coeff.reshape(right_coeff.shape[0], -1).astype(jnp.float32)
    aligned = jnp.dot(matches, flat, precision=lax.Precision.HIGHEST).reshape(right_coeff.shape)
    per_block = jnp.einsum('arc,asc->ars', left_coeff.astype(jnp.float32), aligned, precision=lax.Precision.HIGHEST)
    return jnp.sum(per_block, axis=0)


def reference(coeffs, amplitudes, denominators, pno_count, domains, far_owner, far_pair, near_pair):
    pair_total = coeffs.shape[0]
    live_rows = jnp.arange(NPNO, dtype=jnp.int32)[None, :] < pno_count[:, None]
    live_both = live_rows[:, :, None] & live_rows[:, None, :]
    amp_square = amplitudes.reshape(pair_total, NPNO, NPNO).astype(jnp.float32)
    amp_masked = jnp.where(live_both, amp_square, jnp.zeros((), jnp.float32))
    pair_ids = jnp.arange(pair_total, dtype=jnp.int32)
    device = pair_ids // P_DEV
    owner_occ = device // N_REP
    owner_rep = device % N_REP
    near_ids = (owner_occ[:, None] * (N_REP * P_DEV) + near_pair).astype(jnp.int32)
    far_ids = ((far_owner * N_REP + owner_rep[:, None]) * P_DEV + far_pair).astype(jnp.int32)
    all_ids = jnp.concatenate([near_ids, far_ids], axis=1)

    def masked_coeff(index):
        return jnp.where(live_rows[index][..., None, :, None], coeffs[index], jnp.zeros((), coeffs.dtype))

    def pair_terms(pair_index):
        others = all_ids[pair_index]
        left_coeff = masked_coeff(pair_index)
        intersections = jax.vmap(intersection, in_axes=(None, None, 0, 0))(left_coeff, domains[pair_index], masked_coeff(others), domains[others])
        gain_terms = jnp.einsum('kab,kbc,kdc->ad', intersections, amp_masked[others], intersections, precision=lax.Precision.HIGHEST)
        far_over = intersections[KL:]
        back_terms = jnp.einsum('kba,bc,kcd->kad', far_over, amp_masked[pair_index], far_over, precision=lax.Precision.HIGHEST)
        return gain_terms, back_terms

    gain_terms, back_terms = lax.map(pair_terms, pair_ids)
    back_sum = jax.ops.segment_sum(back_terms.reshape(pair_total * KN, NPNO, NPNO), far_ids.reshape(-1), pair_total)
    denominator_sum = denominators[:, :, None] + denominators[:, None, :]
    residual = denominator_sum * amp_masked + gain_terms + back_sum
    residual = jnp.where(live_both, residual, jnp.zeros((), jnp.float32))
    return residual.reshape(pair_total, NPNO * NPNO)
```

```python
import jax
import jax.numpy as jnp
from jax import lax
from jax.sharding import PartitionSpec as P

NPNO = 64
KN = 2
HI = lax.Precision.HIGHEST


def on_device(coeffs, amplitudes, denominators, pno_count, domains, far_owner, far_pair, near_pair):
    n = coeffs.shape[0]
    domb, npno, blk = coeffs.shape[1:]
    n_occ = lax.axis_size("occ")
    n_rep = lax.axis_size("rep")
    nblk = 32
    occ = lax.axis_index("occ")
    rep = lax.axis_index("rep")
    group = n_rep * n
    live = jnp.arange(npno, dtype=jnp.int32)[None, :] < pno_count[:, None]
    live2 = live[:, :, None] & live[:, None, :]
    amp = jnp.where(live2.reshape(n, -1), amplitudes, jnp.zeros((), jnp.bfloat16))
    gc = lax.all_gather(coeffs, "rep", axis=0, tiled=True)
    ga = lax.all_gather(amp, "rep", axis=0, tiled=True)
    gdom = lax.dynamic_slice_in_dim(domains, occ * group, group, 0)

    def dense(c, dom):
        hot = dom[:, None, :] == jnp.arange(nblk, dtype=jnp.int32)[None, :, None]
        slot = jnp.sum(jnp.where(hot, jnp.arange(domb, dtype=jnp.int32)[None, None, :], 0), axis=2)
        have = jnp.any(hot, axis=2)
        g = c[jnp.arange(c.shape[0])[:, None], slot]
        return jnp.where(have[:, :, None, None], g, jnp.zeros((), jnp.bfloat16))

    gd = dense(gc, gdom)
    hd = lax.dynamic_slice_in_dim(gd, rep * n, n, 0)
    counts = jnp.sum((near_pair[:, :, None] == jnp.arange(group)[None, None, :]).astype(jnp.float32), axis=1)
    S = jnp.einsum("pbrc,qbsc->pqrs", hd, gd, preferred_element_type=jnp.float32)
    gt = ga.reshape(group, npno, npno).astype(jnp.float32)
    U = jnp.einsum("pqab,qbc->pqac", S, gt, precision=HI) * counts[:, :, None, None]
    near = jnp.einsum("pqac,pqdc->pad", U, S, precision=HI)

    rid = (far_owner * n + far_pair).reshape(-1)
    req = rid.shape[0]
    per = domb * npno * blk // (n_occ * 8 * blk)
    sl = coeffs.reshape(n, n_occ, per, 8, blk).transpose(1, 0, 2, 3, 4)
    ta = amp.reshape(n, n_occ, -1).transpose(1, 0, 2)
    rq = lax.all_gather(rid, "occ", axis=0, tiled=False)
    r1 = lax.all_to_all(sl, "occ", 0, 0, tiled=True).reshape(n_occ * n, per, 8, blk)
    rt = lax.all_to_all(ta, "occ", 0, 0, tiled=True).reshape(n_occ * n, -1)
    f = lax.all_to_all(r1[rq], "occ", 0, 0, tiled=True)
    ft = lax.all_to_all(rt[rq], "occ", 0, 0, tiled=True)
    fc = f.transpose(1, 0, 2, 3, 4).reshape(req, domb, npno, blk)
    fT = ft.transpose(1, 0, 2).reshape(req, npno, npno).astype(jnp.float32)
    far_ids = (far_owner.reshape(-1) * n_rep + rep) * n + far_pair.reshape(-1)
    fd = dense(fc, domains[far_ids]).reshape(n, KN, nblk, npno, blk)
    SF = jnp.einsum("pbrc,pkbsc->pkrs", hd, fd, preferred_element_type=jnp.float32)
    UF = jnp.einsum("pkab,pkbc->pkac", SF, fT.reshape(n, KN, npno, npno), precision=HI)
    far = jnp.einsum("pkac,pkdc->pad", UF, SF, precision=HI)
    T = amp.reshape(n, npno, npno).astype(jnp.float32)
    V = jnp.einsum("pab,pkbc->pkac", T, SF, precision=HI)
    back = jnp.einsum("pkab,pkac->pkbc", SF, V, precision=HI).reshape(req, n_occ, -1)
    bk = lax.all_to_all(back.transpose(1, 0, 2), "occ", 0, 0, tiled=True).reshape(n_occ * req, -1)
    hot = (jnp.arange(n_occ * n)[:, None] == rq.reshape(-1)[None, :]).astype(jnp.float32)
    bs = jnp.dot(hot, bk, precision=HI).reshape(n_occ, n, -1)
    bb = lax.all_to_all(bs, "occ", 0, 0, tiled=True).transpose(1, 0, 2).reshape(n, npno, npno)
    den = denominators[:, :, None] + denominators[:, None, :]
    out = jnp.where(live2, den * T + near + far + bb, jnp.zeros((), jnp.float32))
    return out.reshape(n, npno * npno)


def solution(mesh):
    in_specs = (
        P(("occ", "rep"), None, None, None),
        P(("occ", "rep"), None),
        P(("occ", "rep"), None),
        P(("occ", "rep")),
        P(),
        P(("occ", "rep"), None),
        P(("occ", "rep"), None),
        P(("occ", "rep"), None),
    )
    return jax.shard_map(
        on_device, mesh=mesh, in_specs=in_specs, out_specs=P(("occ", "rep"), None), check_vma=False
    )
```

```python
import jax
import jax.numpy as jnp
from jax import lax
from jax.experimental import pallas as pl
from jax.experimental.pallas import tpu as pltpu
from jax.sharding import PartitionSpec as P

MESH = pl.DeviceIdType.MESH
NBLK = 32
KN = 2
BF = jnp.bfloat16
F32 = jnp.float32
NT = (((1,), (1,)), ((), ()))


def split(x):
    hi = x.astype(BF)
    return hi, (x - hi.astype(F32)).astype(BF)


def mm(a, b):
    return jnp.dot(a, b, preferred_element_type=F32)


def mm_nt(a, b):
    return lax.dot_general(a, b, NT, preferred_element_type=F32)


def kernel(
    n_occ, n_rep, n, domb, npno, blk,
    cnt, rids, snear, sfar, counts, coef, coefs, amp, den, ridrow,
    out,
    G, F, R1, SF, GT, RT, ST, FT, RQ, rqs, acc, SH, SL, UH, UL, BD, W, BKs, BKr, BS, BB, X,
    ysend, yrecv, tsend, trecv, p1s, p1r, p2s, p2r, bs, br, lsem,
):
    me = lax.axis_index("occ")
    rep = lax.axis_index("rep")
    right = lax.rem(rep + 1, n_rep)
    left = lax.rem(rep + n_rep - 1, n_rep)
    far2 = lax.rem(rep + 2, n_rep)
    req = n * KN
    group = n * n_rep
    per = domb * npno // 8 // n_occ
    half = n // 2
    lane = lax.broadcasted_iota(jnp.int32, (8, 128), 1)
    sub = lax.broadcasted_iota(jnp.int32, (8, 128), 0)
    low = lane < npno

    def occ_dev(d):
        return {"occ": d}

    def rep_dev(d):
        return {"rep": d}

    barrier = pltpu.get_barrier_semaphore()

    def greet(k, c):
        pl.semaphore_signal(barrier, inc=1, device_id=occ_dev(lax.rem(me + k, n_occ)), device_id_type=MESH)
        return c

    lax.fori_loop(1, n_occ, greet, 0)
    for d in (left, right):
        pl.semaphore_signal(barrier, inc=1, device_id=rep_dev(d), device_id_type=MESH)

    own = pltpu.make_async_copy(
        coef, G.at[pl.ds(rep * n, n), pl.ds(0, domb)], lsem.at[0])
    own.start()
    own1 = pltpu.make_async_copy(
        coefs.at[:, pl.ds(me * per, per)], R1.at[pl.ds(me * n, n)], lsem.at[1])
    own1.start()

    cntv = jnp.zeros((8, 128), jnp.int32)
    for p in range(n):
        cntv = jnp.where(sub == p, cnt[p], cntv)
    col = lax.rem(lane, npno)
    up = lane // npno
    for i in range(npno * npno // 128):
        x = amp[:, 128 * i : 128 * i + 128].astype(F32)
        x = jnp.concatenate([x, jnp.zeros((8 - n, 128), F32)], axis=0)
        live = (2 * i + up < cntv) & (col < cntv)
        GT[rep, pl.ds(8 * i, 8), :] = jnp.where(live, x, 0.0)
    G[:, domb] = jnp.zeros((group, npno, blk), BF)
    F[:, pl.ds(domb * 8, 8)] = jnp.zeros((req, 8, 8, blk), BF)
    RQ[me] = ridrow[...]
    RT[pl.ds(8 * me, 8), :] = GT[rep, pl.ds(8 * me, 8), :]

    pl.semaphore_wait(barrier, n_occ - 1 + 2)

    def plane(k, c):
        d = lax.rem(me + k, n_occ)
        pltpu.make_async_remote_copy(
            ridrow, RQ.at[me], p1s.at[0], p1r.at[0], device_id=occ_dev(d), device_id_type=MESH).start()
        pltpu.make_async_remote_copy(
            GT.at[rep, pl.ds(8 * d, 8)], RT.at[pl.ds(8 * me, 8)], p1s.at[1], p1r.at[1],
            device_id=occ_dev(d), device_id_type=MESH).start()
        pltpu.make_async_remote_copy(
            coefs.at[:, pl.ds(d * per, per)], R1.at[pl.ds(me * n, n)], p1s.at[2], p1r.at[2],
            device_id=occ_dev(d), device_id_type=MESH).start()
        return c

    lax.fori_loop(1, n_occ, plane, 0)

    full = pl.ds(0, domb)

    def ycopy(src, first, dev, s):
        return pltpu.make_async_remote_copy(
            src, G.at[pl.ds(first, half), full], ysend.at[s], yrecv.at[s],
            device_id=rep_dev(dev), device_id_type=MESH)

    sends = []
    s_ra = ycopy(coef.at[pl.ds(0, half)], rep * n, right, 0)
    s_lb = ycopy(coef.at[pl.ds(half, half)], rep * n + half, left, 1)
    s_rb = ycopy(coef.at[pl.ds(half, half)], rep * n + half, right, 2)
    s_la = ycopy(coef.at[pl.ds(0, half)], rep * n, left, 3)
    t_r = pltpu.make_async_remote_copy(
        GT.at[rep], GT.at[rep], tsend.at[0], trecv.at[0], device_id=rep_dev(right), device_id_type=MESH)
    t_l = pltpu.make_async_remote_copy(
        GT.at[rep], GT.at[rep], tsend.at[1], trecv.at[1], device_id=rep_dev(left), device_id_type=MESH)
    for s in (s_ra, s_lb, t_r, t_l, s_rb, s_la):
        s.start()
    sends += [s_ra, s_lb, s_rb, s_la, t_r, t_l]

    def wait_all(ref, sem):
        pltpu.make_async_copy(ref, ref, sem).wait()

    wait_all(RQ.at[pl.ds(0, n_occ - 1)], p1r.at[0])
    table = pltpu.make_async_copy(RQ, rqs, lsem.at[2])
    table.start()
    wait_all(RT.at[pl.ds(0, 8 * (n_occ - 1))], p1r.at[1])
    wait_all(R1.at[pl.ds(0, n * (n_occ - 1))], p1r.at[2])
    own1.wait()
    table.wait()

    def pick(d, j):
        r = rqs[d, 0, lax.rem(d * req + j, 128)]
        return r, r - (r >> 3) * (8 - n)

    for j in range(req):
        r8, r4 = pick(me, j)
        F[j, pl.ds(me * per, per)] = R1[r4]
        FT[pl.ds(8 * me + j, 1), :] = RT[pl.ds(r8, 1), :]

    def gather(d):
        for j in range(req):
            r8, r4 = pick(d, j)
            SF[d, j] = R1[r4]
            ST[pl.ds(8 * d + j, 1), :] = RT[pl.ds(r8, 1), :]

    def ship(d):
        pltpu.make_async_remote_copy(
            SF.at[d], F.at[:, pl.ds(me * per, per)], p2s.at[0], p2r.at[0],
            device_id=occ_dev(d), device_id_type=MESH).start()
        pltpu.make_async_remote_copy(
            ST.at[pl.ds(8 * d, 8)], FT.at[pl.ds(8 * me, 8)], p2s.at[1], p2r.at[1],
            device_id=occ_dev(d), device_id_type=MESH).start()

    gather(lax.rem(me + 1, n_occ))

    def answer(k, c):
        gather(lax.rem(me + k, n_occ))
        ship(lax.rem(me + k - 1, n_occ))
        return c

    lax.fori_loop(2, n_occ, answer, 0)
    ship(lax.rem(me + n_occ - 1, n_occ))

    s_ra.wait_recv()
    f_r = ycopy(G.at[pl.ds(left * n, half), full], left * n, right, 4)
    f_r.start()
    s_lb.wait_recv()
    f_l = ycopy(G.at[pl.ds(right * n + half, half), full], right * n + half, left, 5)
    f_l.start()
    t_r.wait_recv()
    t_l.wait_recv()
    ft = pltpu.make_async_remote_copy(
        GT.at[left], GT.at[left], tsend.at[2], trecv.at[2], device_id=rep_dev(right), device_id_type=MESH)
    ft.start()
    sends += [f_r, f_l, ft]
    s_rb.wait_recv()
    s_la.wait_recv()
    own.wait()
    ft.wait_recv()
    f_r.wait_recv()
    f_l.wait_recv()

    acc[...] = jnp.zeros_like(acc)

    def overlap(b, c):
        hs, gs = [], []
        for t in range(2):
            bb = 2 * b + t
            hs.append(jnp.concatenate(
                [G[rep * n + p, snear[(rep * n + p) * NBLK + bb]] for p in range(n)], axis=0))
            gs.append(jnp.concatenate([G[q, snear[q * NBLK + bb]] for q in range(group)], axis=0))
        acc[...] += mm_nt(jnp.concatenate(hs, axis=1), jnp.concatenate(gs, axis=1))
        return c

    lax.fori_loop(0, NBLK // 2, overlap, 0)

    lane32 = lax.broadcasted_iota(jnp.int32, (npno // 2, 128), 1) < npno

    def place(x, slot, odd):
        other = pltpu.roll(x, npno, 1)
        if odd:
            BD[slot, pl.ds(npno, npno // 2, stride=2), :] = jnp.where(lane32, 0.0, other)
            BD[slot, pl.ds(npno + 1, npno // 2, stride=2), :] = jnp.where(lane32, 0.0, x)
        else:
            BD[slot, pl.ds(0, npno // 2, stride=2), :] = jnp.where(lane32, x, 0.0)
            BD[slot, pl.ds(1, npno // 2, stride=2), :] = jnp.where(lane32, other, 0.0)

    for q in range(group):
        place(GT[q // n, pl.ds(q % n, npno // 2, stride=8), :], q // 2, q % 2)

    low64 = lax.broadcasted_iota(jnp.int32, (npno, 128), 1) < npno

    def project(k, c):
        sl = pl.ds(pl.multiple_of(k * 128, 128), 128)
        hi, lo = split(acc[:, sl])
        SH[:, sl] = hi
        SL[:, sl] = lo
        bd = BD[k].astype(BF)
        u = mm(jnp.concatenate([hi, lo], axis=1), jnp.concatenate([bd, bd], axis=0))
        for p in range(n):
            w = jnp.where(low64, counts[p * group + 2 * k], counts[p * group + 2 * k + 1])
            uh, ul = split(u[p * npno : (p + 1) * npno] * w)
            UH[pl.ds(p * npno, npno), sl] = uh
            UL[pl.ds(p * npno, npno), sl] = ul
        return c

    lax.fori_loop(0, group // 2, project, 0)

    def flat(slot):
        e = W[slot, pl.ds(0, npno // 2, stride=2), :]
        o = W[slot, pl.ds(1, npno // 2, stride=2), :]
        return jnp.where(lane32, e, pltpu.roll(o, npno, 1))

    for p in range(n):
        rows = pl.ds(p * npno, npno)
        g = mm_nt(UH[rows, :], SH[rows, :]) + mm_nt(UL[rows, :], SH[rows, :]) + mm_nt(UH[rows, :], SL[rows, :])
        W[2 * req + p, :, pl.ds(0, npno)] = g

    wait_all(FT.at[pl.ds(0, 8 * (n_occ - 1))], p2r.at[1])
    for j in range(req):
        place(FT[pl.ds(j, npno // 2, stride=8), :], group // 2 + j // 2, j % 2)
    wait_all(F.at[:, pl.ds(0, (n_occ - 1) * per)], p2r.at[0])
    for p in range(n):
        h = jnp.concatenate([G[rep * n + p, a] for a in range(domb)], axis=1)
        f = jnp.concatenate([
            jnp.concatenate([F[KN * p + t, pl.ds(8 * sfar[(KN * p + t) * domb + a], 8)].reshape(npno, blk) for a in range(domb)], axis=1)
            for t in range(KN)], axis=0)
        s = mm_nt(h, f)
        sh, sl_ = split(s)
        bd = BD[group // 2 + p].astype(BF)
        u = mm(jnp.concatenate([sh, sl_], axis=1), jnp.concatenate([bd, bd], axis=0))
        uh, ul = split(u)
        W[2 * req + p, :, pl.ds(0, npno)] += mm_nt(uh, sh) + mm_nt(ul, sh) + mm_nt(uh, sl_)
        odd = p % 2
        tp = BD[rep * (n // 2) + p // 2, pl.ds(odd * npno, npno), :].astype(BF)
        if odd:
            z = jnp.zeros((npno, 128), BF)
            v = mm(tp, jnp.concatenate([z[:npno], sh], axis=0)) + mm(tp, jnp.concatenate([z[:npno], sl_], axis=0))
        else:
            z = jnp.zeros((npno, 128), BF)
            v = mm(tp, jnp.concatenate([sh, z[:npno]], axis=0)) + mm(tp, jnp.concatenate([sl_, z[:npno]], axis=0))
        st = s.T
        th, tl = split(st)
        vh, vl = split(v)
        b = mm(th, vh) + mm(tl, vh) + mm(th, vl)
        W[KN * p, :, :] = b[:npno]
        W[KN * p + 1, :, :] = pltpu.roll(b[npno:], npno, 1)
    for j in range(req):
        BKs[pl.ds(j, npno // 2, stride=8), :] = flat(j)
    for p in range(n):
        X[pl.ds(p, npno // 2, stride=8), :] = flat(2 * req + p)

    def back(src, dst, s):
        def go(k, c):
            d = lax.rem(me + k, n_occ)
            pltpu.make_async_remote_copy(
                src.at[pl.ds(8 * d, 8)], dst.at[pl.ds(8 * me, 8)], bs.at[s], br.at[s],
                device_id=occ_dev(d), device_id_type=MESH).start()
            return c

        lax.fori_loop(1, n_occ, go, 0)
        dst[pl.ds(8 * me, 8), :] = src[pl.ds(8 * me, 8), :]

    rows_in = pl.ds(0, 8 * (n_occ - 1))
    back(BKs, BKr, 0)
    hn = n_occ // 2
    ids = jnp.concatenate(
        [jnp.sum(RQ[pl.ds(h * hn, hn)], axis=0) for h in range(2)], axis=1)
    hot = (lax.broadcasted_iota(jnp.int32, (8 * n_occ, req * n_occ), 0) == ids).astype(F32).astype(BF)
    wait_all(BKr.at[rows_in], br.at[0])
    kh, kl = split(BKr[...])
    BS[...] = mm(hot, kh) + mm(hot, kl)
    back(BS, BB, 1)
    dd = jnp.concatenate([den[...], jnp.zeros((8 - n, npno), F32)], axis=0)
    db = jnp.concatenate([dd, dd], axis=1)
    wait_all(BB.at[rows_in], br.at[1])
    for i in range(npno * npno // 128):
        r = pl.ds(8 * i, 8)
        da = jnp.where(low, dd[:, 2 * i : 2 * i + 1], dd[:, 2 * i + 1 : 2 * i + 2])
        live = (2 * i + up < cntv) & (col < cntv)
        x = (da + db) * GT[rep, r, :] + X[r, :] + BB[r, :]
        out[:, 128 * i : 128 * i + 128] = jnp.where(live, x, 0.0)[:n]

    for s in sends:
        s.wait_send()
    wait_all(RQ.at[pl.ds(0, n_occ - 1)], p1s.at[0])
    wait_all(RT.at[rows_in], p1s.at[1])
    wait_all(R1.at[pl.ds(0, n * (n_occ - 1))], p1s.at[2])
    wait_all(F.at[:, pl.ds(0, (n_occ - 1) * per)], p2s.at[0])
    wait_all(FT.at[rows_in], p2s.at[1])
    wait_all(BKr.at[rows_in], bs.at[0])
    wait_all(BB.at[rows_in], bs.at[1])


def on_device(n_occ, n_rep, coeffs, amplitudes, denominators, pno_count, domains, far_owner, far_pair, near_pair):
    n, domb, npno, blk = coeffs.shape
    occ = lax.axis_index("occ")
    rep = lax.axis_index("rep")
    group = n * n_rep
    req = n * KN
    i32 = jnp.int32
    gdom = lax.dynamic_slice_in_dim(domains, occ * group, group, 0)
    a_id = jnp.arange(domb, dtype=i32) - domb
    hot = gdom[:, None, :] == jnp.arange(NBLK, dtype=i32)[None, :, None]
    snear = (domb + jnp.sum(jnp.where(hot, a_id, 0), axis=2)).reshape(-1)
    far_ids = ((far_owner * n_rep + rep) * n + far_pair).reshape(-1)
    fdom = domains[far_ids]
    hdom = jnp.repeat(lax.dynamic_slice_in_dim(domains, (occ * n_rep + rep) * n, n, 0), KN, axis=0)
    sfar = (domb + jnp.sum(jnp.where(hdom[:, :, None] == fdom[:, None, :], a_id, 0), axis=2)).reshape(-1)
    counts = jnp.sum((near_pair[:, None, :] == jnp.arange(group, dtype=i32)[None, :, None]).astype(F32), axis=2)
    rids = (far_owner * 8 + far_pair).reshape(-1)
    lanes = jnp.arange(128, dtype=i32)
    ridrow = jnp.where(lanes // req == lax.rem(occ, 128 // req), jnp.tile(rids, 128 // req), 0)[None, :]

    smem = pl.BlockSpec(memory_space=pltpu.SMEM)
    vmem = pl.BlockSpec(memory_space=pltpu.VMEM)
    anym = pl.BlockSpec(memory_space=pl.ANY)
    rows = 8 * n_occ
    per = domb * npno // 8 // n_occ
    V = pltpu.VMEM
    dma = pltpu.SemaphoreType.DMA
    import functools
    return pl.pallas_call(
        functools.partial(kernel, n_occ, n_rep, n, domb, npno, blk),
        out_shape=jax.ShapeDtypeStruct((n, npno * npno), F32),
        in_specs=[smem] * 5 + [anym, anym, vmem, vmem, vmem],
        out_specs=vmem,
        scratch_shapes=[
            V((group, domb + 1, npno, blk), BF),
            V((req, (domb + 1) * 8, 8, blk), BF),
            V((n_occ * n, per, 8, blk), BF),
            V((n_occ, req, per, 8, blk), BF),
            V((n_rep, rows, 128), F32),
            V((rows, 128), F32),
            V((rows, 128), F32),
            V((rows, 128), F32),
            V((n_occ, 1, 128), i32),
            pltpu.SMEM((n_occ, 1, 128), i32),
            V((n * npno, group * npno), F32),
            V((n * npno, group * npno), BF),
            V((n * npno, group * npno), BF),
            V((n * npno, group * npno), BF),
            V((n * npno, group * npno), BF),
            V((group // 2 + n, 128, 128), F32),
            V((2 * req + n, npno, 128), F32),
            V((rows, 128), F32),
            V((rows, 128), F32),
            V((rows, 128), F32),
            V((rows, 128), F32),
            V((rows, 128), F32),
            dma((6,)), dma((6,)), dma((3,)), dma((3,)),
            dma((3,)), dma((3,)), dma((2,)), dma((2,)), dma((2,)), dma((2,)), dma((3,)),
        ],
        compiler_params=pltpu.CompilerParams(
            collective_id=0, has_side_effects=True, vmem_limit_bytes=56 * 1024 * 1024),
    )(pno_count, rids, snear, sfar, counts.reshape(-1), coeffs, coeffs.reshape(n, domb * npno // 8, 8, blk),
      amplitudes, denominators, ridrow)


def solution(mesh):
    import functools
    both = ("occ", "rep")
    in_specs = (
        P(both, None, None, None), P(both, None), P(both, None), P(both),
        P(), P(both, None), P(both, None), P(both, None),
    )
    return jax.shard_map(
        functools.partial(on_device, mesh.shape["occ"], mesh.shape["rep"]),
        mesh=mesh, in_specs=in_specs, out_specs=P(both, None), check_vma=False,
    )
```

```python
import functools

import jax
import jax.numpy as jnp
from jax import lax
from jax.experimental import pallas as pl
from jax.experimental.pallas import tpu as pltpu
from jax.sharding import PartitionSpec as P

MESH = pl.DeviceIdType.MESH
NBLK = 32
KN = 2
BF = jnp.bfloat16
F32 = jnp.float32
NT = (((1,), (1,)), ((), ()))


def split(x):
    hi = x.astype(BF)
    return hi, (x - hi.astype(F32)).astype(BF)


def mm(a, b):
    return jnp.dot(a, b, preferred_element_type=F32)


def mm_nt(a, b):
    return lax.dot_general(a, b, NT, preferred_element_type=F32)


def kernel(
    n_occ, n_rep, n, domb, npno, blk, nx, nz,
    cnt, fown, fpair, coef, coefs, amp, den, near, dom,
    out,
    G0, G1, G2, G3, F, R1, SF, T0, TB, TP, GP, GT, RB, RT, ST, SB, FB, FT, RR, RQ, rqs, IV, ivs, acc, BD, W,
    BKs, BKr, BS, BB, X,
    ysend, yrecv, tsend, trecv, p1s, p1r, p2s, p2r, bs, br, lsem,
):
    me = lax.axis_index("occ")
    rep = lax.axis_index("rep")
    cores = n_occ // (nx * nz)
    mx, mz, mc = me // (nz * cores), lax.rem(me // cores, nz), lax.rem(me, cores)
    req = n * KN
    group = n * n_rep
    tiles = npno * npno // 128
    per = domb * npno // 8 // n_occ
    lane = lax.broadcasted_iota(jnp.int32, (8, 128), 1)
    sub = lax.broadcasted_iota(jnp.int32, (8, 128), 0)
    low = lane < npno
    G = (G0, G1, G2, G3)

    def occ_dev(d):
        return {"occ": d}

    def rep_dev(r):
        return {"rep": lax.rem(rep + r, n_rep)}

    def at(dx, dz, dc):
        return (lax.rem(mx + dx, nx) * nz + lax.rem(mz + dz, nz)) * cores + lax.rem(mc + dc, cores)

    def peer(k):
        dx, rest = lax.rem(k, nx), k // nx
        return at(dx, lax.rem(rest + dx, nz), rest // nz)

    def span(d, m):
        return min(d, m - d)

    outward = sorted(
        [(dx, dz, dc) for dc in range(cores) for dz in range(nz) for dx in range(nx) if (dx, dz, dc) != (0, 0, 0)],
        key=lambda o: -(span(o[0], nx) + span(o[1], nz)))

    barrier = pltpu.get_barrier_semaphore()
    for o in outward:
        pl.semaphore_signal(barrier, inc=1, device_id=occ_dev(at(*o)), device_id_type=MESH)
    for r in range(1, n_rep):
        pl.semaphore_signal(barrier, inc=1, device_id=rep_dev(r), device_id_type=MESH)

    blocks = pl.ds(0, domb)
    own = pltpu.make_async_copy(coef, G0.at[:, blocks], lsem.at[0])
    own.start()
    own1 = pltpu.make_async_copy(
        coefs.at[:, pl.ds(me * per, per)], R1.at[pl.ds(me * n, n)], lsem.at[1])
    own1.start()

    rr = jnp.zeros((1, 128), jnp.int32)
    lane1 = lax.broadcasted_iota(jnp.int32, (1, 128), 1)
    base = lax.rem(me * req, 128)
    for j in range(req):
        rr = jnp.where(lane1 == base + j, fown[j // KN, j % KN] * 8 + fpair[j // KN, j % KN], rr)
    RR[...] = rr
    RQ[me] = rr

    cntv = jnp.zeros((8, 128), jnp.int32)
    for p in range(n):
        cntv = jnp.where(sub == p, cnt[p], cntv)
    col = lax.rem(lane, npno)
    up = lane // npno
    pad = jnp.zeros((8 - n, 128), F32)
    last = None
    for i in range(tiles):
        x = jnp.concatenate([amp[:, 128 * i : 128 * i + 128].astype(F32), pad], axis=0)
        live = (2 * i + up < cntv) & (col < cntv)
        x = jnp.where(live, x, 0.0)
        T0[pl.ds(8 * i, 8), :] = x
        TB[i] = x.astype(BF)
        if i % 2:
            TP[i // 2] = (last + pltpu.roll(x, n, 0)).astype(BF)
        last = x

    rows_d = [dom[pl.ds(pl.multiple_of(me * group, group), group), :]]
    for j in range(req):
        owner, pair = fown[j // KN, j % KN], fpair[j // KN, j % KN]
        rows_d.append(dom[pl.ds((owner * n_rep + rep) * n + pair, 1), :])
    dd = jnp.concatenate(rows_d, axis=0)
    lane_i = lax.broadcasted_iota(jnp.int32, (group + req, 128), 1)
    inv = jnp.full((group + req, 128), domb, jnp.int32)
    for a in range(domb):
        inv = jnp.where(dd[:, a : a + 1] == lane_i, a, inv)
    IV[pl.ds(0, group + req), :] = inv
    IV[pl.ds(group + req, group), pl.ds(0, domb)] = dd[:group]

    for g in G:
        g[:, domb] = jnp.zeros((n, npno, blk), BF)
    F[:, pl.ds(domb * 8, 8)] = jnp.zeros((req, 8, 8, blk), BF)
    RB[me] = TB[me]

    pl.semaphore_wait(barrier, n_occ - 1 + n_rep - 1)
    index = pltpu.make_async_copy(IV, ivs, lsem.at[3])
    index.start()

    def plane(k, c):
        d = peer(k)
        pltpu.make_async_remote_copy(
            RR, RQ.at[me], p1s.at[0], p1r.at[0], device_id=occ_dev(d), device_id_type=MESH).start()
        pltpu.make_async_remote_copy(
            TB.at[d], RB.at[me], p1s.at[1], p1r.at[1], device_id=occ_dev(d), device_id_type=MESH).start()
        pltpu.make_async_remote_copy(
            coefs.at[:, pl.ds(d * per, per)], R1.at[pl.ds(me * n, n)], p1s.at[2], p1r.at[2],
            device_id=occ_dev(d), device_id_type=MESH).start()
        return c

    lax.fori_loop(1, n_occ, plane, 0)

    sends = {}
    for r in sorted(range(1, n_rep), key=lambda r: span(r, n_rep)):
        to = n_rep - r
        t = pltpu.make_async_remote_copy(
            TP, GP.at[to], tsend.at[r], trecv.at[to], device_id=rep_dev(r), device_id_type=MESH)
        c = pltpu.make_async_remote_copy(
            coef, G[to].at[:, blocks], ysend.at[r], yrecv.at[to], device_id=rep_dev(r), device_id_type=MESH)
        t.start()
        c.start()
        sends[r] = (t, c)

    def wait_all(ref, sem):
        pltpu.make_async_copy(ref, ref, sem).wait()

    index.wait()
    own.wait()
    GP[0] = TP[...]
    lane32 = lax.broadcasted_iota(jnp.int32, (npno // 2, 128), 1) < npno
    low64 = lax.broadcasted_iota(jnp.int32, (npno, 128), 1) < npno

    def place(x, slot, odd):
        other = pltpu.roll(x, npno, 1)
        if odd:
            BD[slot, pl.ds(npno, npno // 2, stride=2), :] = jnp.where(lane32, 0.0, other)
            BD[slot, pl.ds(npno + 1, npno // 2, stride=2), :] = jnp.where(lane32, 0.0, x)
        else:
            BD[slot, pl.ds(0, npno // 2, stride=2), :] = jnp.where(lane32, x, 0.0)
            BD[slot, pl.ds(1, npno // 2, stride=2), :] = jnp.where(lane32, other, 0.0)

    def near_part(r, gains):
        dev = lax.rem(rep + r, n_rep)
        acc[...] = jnp.zeros_like(acc)

        def overlap(b, c):
            hs, gs = [], []
            for t in range(4):
                bb = 4 * b + t
                hs.append(jnp.concatenate([G0[p, ivs[rep * n + p, bb]] for p in range(n)], axis=0))
                gs.append(jnp.concatenate([G[r][q, ivs[dev * n + q, bb]] for q in range(n)], axis=0))
            acc[...] += mm_nt(jnp.concatenate(hs, axis=1), jnp.concatenate(gs, axis=1))
            return c

        lax.fori_loop(0, NBLK // 4, overlap, 0)
        GT[...] = GP[r].astype(F32).reshape(n * tiles, 128)
        for q in range(n):
            place(GT[pl.ds(q, npno // 2, stride=n), :], (n * r + q) // 2, q % 2)
        parts = [[] for _ in range(n)]
        for k in range(n // 2):
            hi, lo = split(acc[:, 128 * k : 128 * k + 128])
            bd = BD[n // 2 * r + k].astype(BF)
            u = mm(jnp.concatenate([hi, lo], axis=1), jnp.concatenate([bd, bd], axis=0))
            q = dev * n + 2 * k
            c0 = jnp.sum((near[...] == q).astype(F32), axis=1, keepdims=True)
            c1 = jnp.sum((near[...] == q + 1).astype(F32), axis=1, keepdims=True)
            w = jnp.where(low[:n], c0, c1)
            for p in range(n):
                rows = slice(p * npno, (p + 1) * npno)
                uh, ul = split(u[rows] * w[p : p + 1])
                parts[p].append((uh, ul, hi[rows], lo[rows]))
        for p in range(n):
            uh, ul, sh, sl = (jnp.concatenate(v, axis=1) for v in zip(*parts[p]))
            g = mm_nt(uh, sh) + mm_nt(ul, sh) + mm_nt(uh, sl)
            if gains:
                g = g + W[2 * req + p, :, pl.ds(0, npno)]
            W[2 * req + p, :, pl.ds(0, npno)] = g

    near_part(0, False)

    wait_all(RQ.at[pl.ds(0, n_occ - 1)], p1r.at[0])
    table = pltpu.make_async_copy(RQ, rqs, lsem.at[2])
    table.start()
    wait_all(RB.at[pl.ds(0, n_occ - 1)], p1r.at[1])
    RT[...] = RB[...].astype(F32).reshape(8 * n_occ, 128)
    wait_all(R1.at[pl.ds(0, n * (n_occ - 1))], p1r.at[2])
    own1.wait()
    table.wait()

    def pick(d, j):
        r = rqs[d, 0, lax.rem(d * req + j, 128)]
        return r, r - (r >> 3) * (8 - n)

    for j in range(req):
        r8, r4 = pick(me, j)
        F[j, pl.ds(me * per, per)] = R1[r4]
        ST[pl.ds(8 * me + j, 1), :] = RT[pl.ds(r8, 1), :]
    FB[me] = ST[pl.ds(8 * me, 8), :].astype(BF)

    def gather(d):
        for j in range(req):
            r8, r4 = pick(d, j)
            SF[d, j] = R1[r4]
            ST[pl.ds(8 * d + j, 1), :] = RT[pl.ds(r8, 1), :]
        SB[d] = ST[pl.ds(8 * d, 8), :].astype(BF)

    def ship(d):
        pltpu.make_async_remote_copy(
            SF.at[d], F.at[:, pl.ds(me * per, per)], p2s.at[0], p2r.at[0],
            device_id=occ_dev(d), device_id_type=MESH).start()
        pltpu.make_async_remote_copy(
            SB.at[d], FB.at[me], p2s.at[1], p2r.at[1],
            device_id=occ_dev(d), device_id_type=MESH).start()

    gather(peer(1))

    def answer(k, c):
        gather(peer(k))
        ship(peer(k - 1))
        return c

    lax.fori_loop(2, n_occ, answer, 0)
    ship(peer(n_occ - 1))

    for r in sorted(range(1, n_rep), key=lambda r: span(r, n_rep)):
        for c in sends[n_rep - r]:
            c.wait_recv()
        near_part(r, True)

    wait_all(FB.at[pl.ds(0, n_occ - 1)], p2r.at[1])
    FT[...] = FB[...].astype(F32).reshape(8 * n_occ, 128)
    for j in range(req):
        place(FT[pl.ds(j, npno // 2, stride=8), :], (group + j) // 2, j % 2)
    wait_all(F.at[:, pl.ds(0, (n_occ - 1) * per)], p2r.at[0])

    def flat(slot):
        e = W[slot, pl.ds(0, npno // 2, stride=2), :]
        o = W[slot, pl.ds(1, npno // 2, stride=2), :]
        return jnp.where(lane32, e, pltpu.roll(o, npno, 1))

    z = jnp.zeros((npno, 128), BF)
    for p in range(n):
        h = jnp.concatenate([G0[p, a] for a in range(domb)], axis=1)
        f = jnp.concatenate([
            jnp.concatenate([
                F[j, pl.ds(8 * ivs[group + j, ivs[group + req + rep * n + p, a]], 8)].reshape(npno, blk)
                for a in range(domb)], axis=1)
            for j in range(KN * p, KN * p + KN)], axis=0)
        s = mm_nt(h, f)
        sh, sl = split(s)
        th, tl = split(s.T)
        bd = BD[group // 2 + p].astype(BF)
        u = mm(jnp.concatenate([sh, sl], axis=1), jnp.concatenate([bd, bd], axis=0))
        odd = p % 2
        tp = BD[p // 2, pl.ds(odd * npno, npno), :].astype(BF)
        v = mm(jnp.concatenate([tp, tp], axis=1),
               jnp.concatenate([z, sh, z, sl] if odd else [sh, z, sl, z], axis=0))
        vh, vl = split(v)
        b = mm(th, vh) + mm(tl, vh) + mm(th, vl)
        W[KN * p, :, :] = b[:npno]
        W[KN * p + 1, :, :] = pltpu.roll(b[npno:], npno, 1)
        uh, ul = split(u)
        W[2 * req + p, :, pl.ds(0, npno)] += mm_nt(uh, sh) + mm_nt(ul, sh) + mm_nt(uh, sl)
    for j in range(req):
        BKs[pl.ds(j, npno // 2, stride=8), :] = flat(j)

    def back(src, dst, s):
        for o in outward:
            d = at(*o)
            pltpu.make_async_remote_copy(
                src.at[pl.ds(8 * d, 8)], dst.at[pl.ds(8 * me, 8)], bs.at[s], br.at[s],
                device_id=occ_dev(d), device_id_type=MESH).start()
        dst[pl.ds(8 * me, 8), :] = src[pl.ds(8 * me, 8), :]

    rows_in = pl.ds(0, 8 * (n_occ - 1))
    back(BKs, BKr, 0)
    hn = n_occ // 2
    ids = jnp.concatenate(
        [jnp.sum(RQ[pl.ds(h * hn, hn)], axis=0) for h in range(2)], axis=1)
    hot = (lax.broadcasted_iota(jnp.int32, (8 * n_occ, req * n_occ), 0) == ids).astype(F32).astype(BF)
    for p in range(n):
        X[pl.ds(p, npno // 2, stride=8), :] = flat(2 * req + p)
    de = jnp.concatenate([den[...], jnp.zeros((8 - n, npno), F32)], axis=0)
    db = jnp.concatenate([de, de], axis=1)
    for i in range(tiles):
        r = pl.ds(8 * i, 8)
        da = jnp.where(low, de[:, 2 * i : 2 * i + 1], de[:, 2 * i + 1 : 2 * i + 2])
        X[r, :] = (da + db) * T0[r, :] + X[r, :]
    wait_all(BKr.at[rows_in], br.at[0])
    kh, kl = split(BKr[...])
    BS[...] = mm(hot, kh) + mm(hot, kl)
    back(BS, BB, 1)
    wait_all(BB.at[rows_in], br.at[1])
    for i in range(tiles):
        r = pl.ds(8 * i, 8)
        live = (2 * i + up < cntv) & (col < cntv)
        out[:, 128 * i : 128 * i + 128] = jnp.where(live, X[r, :] + BB[r, :], 0.0)[:n]

    for r in range(1, n_rep):
        for c in sends[r]:
            c.wait_send()
    wait_all(RQ.at[pl.ds(0, n_occ - 1)], p1s.at[0])
    wait_all(RB.at[pl.ds(0, n_occ - 1)], p1s.at[1])
    wait_all(R1.at[pl.ds(0, n * (n_occ - 1))], p1s.at[2])
    wait_all(F.at[:, pl.ds(0, (n_occ - 1) * per)], p2s.at[0])
    wait_all(FB.at[pl.ds(0, n_occ - 1)], p2s.at[1])
    wait_all(BKr.at[rows_in], bs.at[0])
    wait_all(BB.at[rows_in], bs.at[1])


def on_device(n_occ, n_rep, coeffs, amplitudes, denominators, pno_count, domains, far_owner, far_pair, near_pair):
    n, domb, npno, blk = coeffs.shape
    group = n * n_rep
    req = n * KN
    i32 = jnp.int32
    smem = pl.BlockSpec(memory_space=pltpu.SMEM)
    vmem = pl.BlockSpec(memory_space=pltpu.VMEM)
    anym = pl.BlockSpec(memory_space=pl.ANY)
    rows = 8 * n_occ
    per = domb * npno // 8 // n_occ
    tiles = npno * npno // 128
    V = pltpu.VMEM
    dma = pltpu.SemaphoreType.DMA
    return pl.pallas_call(
        functools.partial(kernel, n_occ, n_rep, n, domb, npno, blk, 4, 4),
        out_shape=jax.ShapeDtypeStruct((n, npno * npno), F32),
        in_specs=[smem] * 3 + [anym, anym] + [vmem] * 4,
        out_specs=vmem,
        scratch_shapes=[V((n, domb + 1, npno, blk), BF)] * 4 + [
            V((req, (domb + 1) * 8, 8, blk), BF),
            V((n_occ * n, per, 8, blk), BF),
            V((n_occ, req, per, 8, blk), BF),
            V((rows, 128), F32),
            V((n_occ, 8, 128), BF),
            V((tiles // 2, 8, 128), BF),
            V((n_rep, tiles // 2, 8, 128), BF),
            V((n * tiles, 128), F32),
            V((n_occ, 8, 128), BF),
            V((rows, 128), F32),
            V((rows, 128), F32),
            V((n_occ, 8, 128), BF),
            V((n_occ, 8, 128), BF),
            V((rows, 128), F32),
            V((1, 128), i32),
            V((n_occ, 1, 128), i32),
            pltpu.SMEM((n_occ, 1, 128), i32),
            V((2 * group + req, 128), i32),
            pltpu.SMEM((2 * group + req, 128), i32),
            V((n * npno, n * npno), F32),
            V((group // 2 + n, 128, 128), F32),
            V((2 * req + n, npno, 128), F32),
            V((rows, 128), F32),
            V((rows, 128), F32),
            V((rows, 128), F32),
            V((rows, 128), F32),
            V((rows, 128), F32),
            dma((n_rep,)), dma((n_rep,)), dma((n_rep,)), dma((n_rep,)),
            dma((3,)), dma((3,)), dma((2,)), dma((2,)), dma((2,)), dma((2,)), dma((4,)),
        ],
        compiler_params=pltpu.CompilerParams(
            collective_id=0, has_side_effects=True, vmem_limit_bytes=56 * 1024 * 1024),
    )(pno_count, far_owner, far_pair, coeffs, coeffs.reshape(n, domb * npno // 8, 8, blk),
      amplitudes, denominators, near_pair, domains)


def solution(mesh):
    both = ("occ", "rep")
    in_specs = (
        P(both, None, None, None), P(both, None), P(both, None), P(both),
        P(), P(both, None), P(both, None), P(both, None),
    )
    return jax.shard_map(
        functools.partial(on_device, mesh.shape["occ"], mesh.shape["rep"]),
        mesh=mesh, in_specs=in_specs, out_specs=P(both, None), check_vma=False,
    )
```

```python
import functools

import jax
import jax.numpy as jnp
from jax import lax
from jax.experimental import pallas as pl
from jax.experimental.pallas import tpu as pltpu
from jax.sharding import PartitionSpec as P

MESH = pl.DeviceIdType.MESH
NBLK = 32
KN = 2
BF = jnp.bfloat16
F32 = jnp.float32
NT = (((1,), (1,)), ((), ()))


def split(x):
    hi = x.astype(BF)
    return hi, (x - hi.astype(F32)).astype(BF)


def mm(a, b):
    return jnp.dot(a, b, preferred_element_type=F32)


def mm_nt(a, b):
    return lax.dot_general(a, b, NT, preferred_element_type=F32)


def kernel(
    n_occ, n_rep, n, domb, npno, blk, nx, nz,
    cnt, fown, fpair, coef, coefs, amp, den, near, dom,
    out,
    G0, G1, G2, G3, F, PS, R1, SF, T0, TP, GP, GT, RT, ST, FT, RR, RQ, rqs, DT, IV, ivs, acc, BD, W,
    BKs, BKr, BS, BB, X,
    ysend, yrecv, tsend, trecv, p1s, p1r, p2s, p2r, bs, br, lsem,
):
    me = lax.axis_index("occ")
    rep = lax.axis_index("rep")
    cores = n_occ // (nx * nz)
    mx, mz, mc = me // (nz * cores), lax.rem(me // cores, nz), lax.rem(me, cores)
    req = n * KN
    group = n * n_rep
    tiles = npno * npno // 128
    per = domb * npno // 8 // n_occ
    lane = lax.broadcasted_iota(jnp.int32, (8, 128), 1)
    sub = lax.broadcasted_iota(jnp.int32, (8, 128), 0)
    low = lane < npno
    G = (G0, G1, G2, G3)

    def occ_dev(d):
        return {"occ": d}

    def rep_dev(r):
        return {"rep": lax.rem(rep + r, n_rep)}

    def at(dx, dz, dc):
        return (lax.rem(mx + dx, nx) * nz + lax.rem(mz + dz, nz)) * cores + lax.rem(mc + dc, cores)

    def peer(k):
        dx, rest = lax.rem(k, nx), k // nx
        return at(dx, lax.rem(rest + dx, nz), rest // nz)

    def span(d, m):
        return min(d, m - d)

    outward = sorted(
        [(dx, dz, dc) for dc in range(cores) for dz in range(nz) for dx in range(nx) if (dx, dz, dc) != (0, 0, 0)],
        key=lambda o: -(span(o[0], nx) + span(o[1], nz)))

    barrier = pltpu.get_barrier_semaphore()
    for o in outward:
        pl.semaphore_signal(barrier, inc=1, device_id=occ_dev(at(*o)), device_id_type=MESH)
    for r in range(1, n_rep):
        pl.semaphore_signal(barrier, inc=1, device_id=rep_dev(r), device_id_type=MESH)

    blocks = pl.ds(0, domb)
    own = pltpu.make_async_copy(coef, G0.at[:, blocks], lsem.at[0])
    own.start()
    cuts = [
        pltpu.make_async_copy(coefs.at[p, t], PS.at[:, per * p + t], lsem.at[4 + per * p + t])
        for p in range(n) for t in range(per)]
    for c in cuts:
        c.start()

    rr = jnp.zeros((1, 128), jnp.int32)
    lane1 = lax.broadcasted_iota(jnp.int32, (1, 128), 1)
    base = lax.rem(me * req, 128)
    for j in range(req):
        rr = jnp.where(lane1 == base + j, fown[j % KN, j // KN] * 8 + fpair[j % KN, j // KN], rr)
    RR[...] = rr
    RQ[me] = rr

    cntv = jnp.zeros((8, 128), jnp.int32)
    for p in range(n):
        cntv = jnp.where(sub == p, cnt[p], cntv)
    col = lax.rem(lane, npno)
    up = lane // npno
    pad = jnp.zeros((8 - n, 128), F32)
    last = None
    for i in range(tiles):
        x = jnp.concatenate([amp[:, 128 * i : 128 * i + 128].astype(F32), pad], axis=0)
        live = (2 * i + up < cntv) & (col < cntv)
        x = jnp.where(live, x, 0.0)
        T0[pl.ds(8 * i, 8), :] = x
        PS[i, n * per] = x.astype(BF)
        if i % 2:
            TP[i // 2] = (last + pltpu.roll(x, n, 0)).astype(BF)
        last = x

    dt = jnp.concatenate([dom[...], jnp.zeros((-domb % 8, dom.shape[1]), jnp.int32)], axis=0)
    DT[...] = dt.T
    rows_d = [DT[pl.ds(pl.multiple_of(me * group, group), group), :]]
    for j in range(req):
        owner, pair = fown[j % KN, j // KN], fpair[j % KN, j // KN]
        rows_d.append(DT[pl.ds((owner * n_rep + rep) * n + pair, 1), :])
    dd = jnp.concatenate(rows_d, axis=0)
    lane_i = lax.broadcasted_iota(jnp.int32, (group + req, 128), 1)
    inv = jnp.full((group + req, 128), domb, jnp.int32)
    for a in range(domb):
        inv = jnp.where(dd[:, a : a + 1] == lane_i, a, inv)
    IV[pl.ds(0, group), :] = inv[:group]
    fi = inv[group:]
    have = fi < domb
    IV[pl.ds(group, req), :] = jnp.where(have, lax.rem(fi * 8, n_occ), n_occ)
    IV[pl.ds(group + req, req), :] = jnp.where(have, (fi * 8) // n_occ, 0)
    IV[pl.ds(group + 2 * req, group), pl.ds(0, dd.shape[1])] = dd[:group]

    for g in G:
        g[:, domb] = jnp.zeros((n, npno, blk), BF)
    for j in range(req):
        F[pl.ds(n_occ, 8), per * j] = jnp.zeros((8, 8, blk), BF)
    for c in cuts:
        c.wait()
    R1[me] = PS[me]

    pl.semaphore_wait(barrier, n_occ - 1 + n_rep - 1)
    index = pltpu.make_async_copy(IV, ivs, lsem.at[3])
    index.start()

    half = n // 2
    ahead, behind = 1, n_rep - 1
    opposite = n_rep // 2

    def halfway(src, h, to, r, s):
        return pltpu.make_async_remote_copy(
            src, G[to].at[pl.ds(h * half, half), blocks], ysend.at[s], yrecv.at[s],
            device_id=rep_dev(r), device_id_type=MESH)

    firsts = [
        halfway(coef.at[pl.ds(0, half)], 0, behind, ahead, 0),
        halfway(coef.at[pl.ds(half, half)], 1, ahead, behind, 1),
        halfway(coef.at[pl.ds(half, half)], 1, behind, ahead, 2),
        halfway(coef.at[pl.ds(0, half)], 0, ahead, behind, 3)]
    relays = [
        halfway(G[behind].at[pl.ds(0, half), blocks], 0, opposite, ahead, 4),
        halfway(G[ahead].at[pl.ds(half, half), blocks], 1, opposite, behind, 5)]
    firsts[0].start()
    firsts[1].start()
    amps = []
    for r in range(1, n_rep):
        t = pltpu.make_async_remote_copy(
            TP, GP.at[n_rep - r], tsend.at[r], trecv.at[n_rep - r], device_id=rep_dev(r), device_id_type=MESH)
        t.start()
        amps.append(t)
    firsts[2].start()
    firsts[3].start()

    def slices(o):
        d = at(*o)
        pltpu.make_async_remote_copy(
            PS.at[d], R1.at[me], p1s.at[1], p1r.at[1], device_id=occ_dev(d), device_id_type=MESH).start()

    for o in outward[:8]:
        slices(o)
    for o in outward:
        pltpu.make_async_remote_copy(
            RR, RQ.at[me], p1s.at[0], p1r.at[0], device_id=occ_dev(at(*o)), device_id_type=MESH).start()
    for o in outward[8:]:
        slices(o)

    def wait_all(ref, sem):
        pltpu.make_async_copy(ref, ref, sem).wait()

    index.wait()
    own.wait()
    GP[0] = TP[...]
    lane32 = lax.broadcasted_iota(jnp.int32, (npno // 2, 128), 1) < npno
    low64 = lax.broadcasted_iota(jnp.int32, (npno, 128), 1) < npno

    def place(x, slot, odd):
        other = pltpu.roll(x, npno, 1)
        if odd:
            BD[slot, pl.ds(npno, npno // 2, stride=2), :] = jnp.where(lane32, 0.0, other)
            BD[slot, pl.ds(npno + 1, npno // 2, stride=2), :] = jnp.where(lane32, 0.0, x)
        else:
            BD[slot, pl.ds(0, npno // 2, stride=2), :] = jnp.where(lane32, x, 0.0)
            BD[slot, pl.ds(1, npno // 2, stride=2), :] = jnp.where(lane32, other, 0.0)

    def near_part(r, gains):
        dev = lax.rem(rep + r, n_rep)
        acc[...] = jnp.zeros_like(acc)

        def overlap(b, c):
            hs, gs = [], []
            for t in range(4):
                bb = 4 * b + t
                hs.append(jnp.concatenate([G0[p, ivs[rep * n + p, bb]] for p in range(n)], axis=0))
                gs.append(jnp.concatenate([G[r][q, ivs[dev * n + q, bb]] for q in range(n)], axis=0))
            acc[...] += mm_nt(jnp.concatenate(hs, axis=1), jnp.concatenate(gs, axis=1))
            return c

        lax.fori_loop(0, NBLK // 4, overlap, 0)
        GT[...] = GP[r].astype(F32).reshape(n * tiles, 128)
        for q in range(n):
            place(GT[pl.ds(q, npno // 2, stride=n), :], (n * r + q) // 2, q % 2)
        parts = [[] for _ in range(n)]
        for k in range(n // 2):
            hi, lo = split(acc[:, 128 * k : 128 * k + 128])
            bd = BD[n // 2 * r + k].astype(BF)
            u = mm(jnp.concatenate([hi, lo], axis=1), jnp.concatenate([bd, bd], axis=0))
            q = dev * n + 2 * k
            c0 = jnp.sum((near[...] == q).astype(F32), axis=1, keepdims=True)
            c1 = jnp.sum((near[...] == q + 1).astype(F32), axis=1, keepdims=True)
            w = jnp.where(low[:n], c0, c1)
            for p in range(n):
                rows = slice(p * npno, (p + 1) * npno)
                uh, ul = split(u[rows] * w[p : p + 1])
                parts[p].append((uh, ul, hi[rows], lo[rows]))
        for p in range(n):
            uh, ul, sh, sl = (jnp.concatenate(v, axis=1) for v in zip(*parts[p]))
            g = mm_nt(uh, sh) + mm_nt(ul, sh) + mm_nt(uh, sl)
            if gains:
                g = g + W[2 * req + p, :, pl.ds(0, npno)]
            W[2 * req + p, :, pl.ds(0, npno)] = g

    near_part(0, False)

    wait_all(RQ.at[pl.ds(0, n_occ - 1)], p1r.at[0])
    table = pltpu.make_async_copy(RQ, rqs, lsem.at[2])
    table.start()
    wait_all(R1.at[pl.ds(0, n_occ - 1)], p1r.at[1])
    RT[...] = R1[:, n * per].astype(F32).reshape(8 * n_occ, 128)
    table.wait()

    def gather(d, dst, at_d):
        for j in range(req):
            r = rqs[d, 0, lax.rem(d * req + j, 128)]
            dst[at_d, pl.ds(per * j, per)] = R1[r >> 3, pl.ds(per * (r & 7), per)]
            ST[pl.ds(8 * d + j, 1), :] = RT[pl.ds(r, 1), :]
        dst[at_d, req * per] = ST[pl.ds(8 * d, 8), :].astype(BF)

    def ship(d):
        pltpu.make_async_remote_copy(
            SF.at[d], F.at[me], p2s.at[0], p2r.at[0], device_id=occ_dev(d), device_id_type=MESH).start()

    gather(peer(1), SF, peer(1))

    def answer(k, c):
        gather(peer(k), SF, peer(k))
        ship(peer(k - 1))
        return c

    lax.fori_loop(2, n_occ, answer, 0)
    ship(peer(n_occ - 1))
    gather(me, F, me)

    for t in range(2):
        firsts[t].wait_recv()
        relays[t].start()
    for t in amps:
        t.wait_recv()
    firsts[3].wait_recv()
    near_part(ahead, True)
    firsts[2].wait_recv()
    near_part(behind, True)
    for t in relays:
        t.wait_recv()
    near_part(opposite, True)

    wait_all(F.at[pl.ds(0, n_occ - 1)], p2r.at[0])
    FT[...] = F[pl.ds(0, n_occ), req * per].astype(F32).reshape(8 * n_occ, 128)
    for j in range(req):
        place(FT[pl.ds(j, npno // 2, stride=8), :], (group + j) // 2, j % 2)

    def flat(slot):
        e = W[slot, pl.ds(0, npno // 2, stride=2), :]
        o = W[slot, pl.ds(1, npno // 2, stride=2), :]
        return jnp.where(lane32, e, pltpu.roll(o, npno, 1))

    def block(j, p, a):
        b = ivs[group + 2 * req + rep * n + p, a]
        return F[pl.ds(ivs[group + j, b], 8), per * j + ivs[group + req + j, b]].reshape(npno, blk)

    z = jnp.zeros((npno, 128), BF)
    for p in range(n):
        h = jnp.concatenate([G0[p, a] for a in range(domb)], axis=1)
        f = jnp.concatenate([
            jnp.concatenate([block(j, p, a) for a in range(domb)], axis=1)
            for j in range(KN * p, KN * p + KN)], axis=0)
        s = mm_nt(h, f)
        sh, sl = split(s)
        th, tl = split(s.T)
        bd = BD[group // 2 + p].astype(BF)
        u = mm(jnp.concatenate([sh, sl], axis=1), jnp.concatenate([bd, bd], axis=0))
        odd = p % 2
        tp = BD[p // 2, pl.ds(odd * npno, npno), :].astype(BF)
        v = mm(jnp.concatenate([tp, tp], axis=1),
               jnp.concatenate([z, sh, z, sl] if odd else [sh, z, sl, z], axis=0))
        vh, vl = split(v)
        b = mm(th, vh) + mm(tl, vh) + mm(th, vl)
        W[KN * p, :, :] = b[:npno]
        W[KN * p + 1, :, :] = pltpu.roll(b[npno:], npno, 1)
        uh, ul = split(u)
        W[2 * req + p, :, pl.ds(0, npno)] += mm_nt(uh, sh) + mm_nt(ul, sh) + mm_nt(uh, sl)
    for j in range(req):
        BKs[pl.ds(j, npno // 2, stride=8), :] = flat(j)

    def back(src, dst, s):
        for o in outward:
            d = at(*o)
            pltpu.make_async_remote_copy(
                src.at[pl.ds(8 * d, 8)], dst.at[pl.ds(8 * me, 8)], bs.at[s], br.at[s],
                device_id=occ_dev(d), device_id_type=MESH).start()
        dst[pl.ds(8 * me, 8), :] = src[pl.ds(8 * me, 8), :]

    rows_in = pl.ds(0, 8 * (n_occ - 1))
    back(BKs, BKr, 0)
    hn = n_occ // 2
    ids = jnp.concatenate(
        [jnp.sum(RQ[pl.ds(h * hn, hn)], axis=0) for h in range(2)], axis=1)
    hot = (lax.broadcasted_iota(jnp.int32, (8 * n_occ, req * n_occ), 0) == ids).astype(F32).astype(BF)
    for p in range(n):
        X[pl.ds(p, npno // 2, stride=8), :] = flat(2 * req + p)
    de = jnp.concatenate([den[...], jnp.zeros((8 - n, npno), F32)], axis=0)
    db = jnp.concatenate([de, de], axis=1)
    for i in range(tiles):
        r = pl.ds(8 * i, 8)
        da = jnp.where(low, de[:, 2 * i : 2 * i + 1], de[:, 2 * i + 1 : 2 * i + 2])
        X[r, :] = (da + db) * T0[r, :] + X[r, :]
    wait_all(BKr.at[rows_in], br.at[0])
    kh, kl = split(BKr[...])
    BS[...] = mm(hot, kh) + mm(hot, kl)
    back(BS, BB, 1)
    wait_all(BB.at[rows_in], br.at[1])
    for i in range(tiles):
        r = pl.ds(8 * i, 8)
        live = (2 * i + up < cntv) & (col < cntv)
        out[:, 128 * i : 128 * i + 128] = jnp.where(live, X[r, :] + BB[r, :], 0.0)[:n]

    for c in firsts + relays + amps:
        c.wait_send()
    wait_all(RQ.at[pl.ds(0, n_occ - 1)], p1s.at[0])
    wait_all(R1.at[pl.ds(0, n_occ - 1)], p1s.at[1])
    wait_all(F.at[pl.ds(0, n_occ - 1)], p2s.at[0])
    wait_all(BKr.at[rows_in], bs.at[0])
    wait_all(BB.at[rows_in], bs.at[1])


def on_device(n_occ, n_rep, coeffs, amplitudes, denominators, pno_count, domains, far_owner, far_pair, near_pair):
    n, domb, npno, blk = coeffs.shape
    group = n * n_rep
    req = n * KN
    i32 = jnp.int32
    smem = pl.BlockSpec(memory_space=pltpu.SMEM)
    vmem = pl.BlockSpec(memory_space=pltpu.VMEM)
    anym = pl.BlockSpec(memory_space=pl.ANY)
    rows = 8 * n_occ
    per = domb * npno // 8 // n_occ
    tiles = npno * npno // 128
    V = pltpu.VMEM
    dma = pltpu.SemaphoreType.DMA
    return pl.pallas_call(
        functools.partial(kernel, n_occ, n_rep, n, domb, npno, blk, 4, 4),
        out_shape=jax.ShapeDtypeStruct((n, npno * npno), F32),
        in_specs=[smem] * 3 + [anym, anym] + [vmem] * 4,
        out_specs=vmem,
        scratch_shapes=[V((n, domb + 1, npno, blk), BF)] * 4 + [
            V((n_occ + 8, req * per + 1, 8, blk), BF),
            V((n_occ, n * per + 1, 8, blk), BF),
            V((n_occ, n * per + 1, 8, blk), BF),
            V((n_occ, req * per + 1, 8, blk), BF),
            V((rows, 128), F32),
            V((tiles // 2, 8, 128), BF),
            V((n_rep, tiles // 2, 8, 128), BF),
            V((n * tiles, 128), F32),
            V((rows, 128), F32),
            V((rows, 128), F32),
            V((rows, 128), F32),
            V((1, 128), i32),
            V((n_occ, 1, 128), i32),
            pltpu.SMEM((n_occ, 1, 128), i32),
            V((domains.shape[0], domb + -domb % 8), i32),
            V((2 * group + 2 * req, 128), i32),
            pltpu.SMEM((2 * group + 2 * req, 128), i32),
            V((n * npno, n * npno), F32),
            V((group // 2 + n, 128, 128), F32),
            V((2 * req + n, npno, 128), F32),
            V((rows, 128), F32),
            V((rows, 128), F32),
            V((rows, 128), F32),
            V((rows, 128), F32),
            V((rows, 128), F32),
            dma((6,)), dma((6,)), dma((n_rep,)), dma((n_rep,)),
            dma((2,)), dma((2,)), dma((1,)), dma((1,)), dma((2,)), dma((2,)), dma((4 + n * per,)),
        ],
        compiler_params=pltpu.CompilerParams(
            collective_id=0, has_side_effects=True, vmem_limit_bytes=56 * 1024 * 1024),
    )(pno_count, far_owner.T, far_pair.T, coeffs, coeffs.reshape(n, per, n_occ, 8, blk),
      amplitudes, denominators, near_pair, domains.T)


def solution(mesh):
    both = ("occ", "rep")
    in_specs = (
        P(both, None, None, None), P(both, None), P(both, None), P(both),
        P(), P(both, None), P(both, None), P(both, None),
    )
    return jax.shard_map(
        functools.partial(on_device, mesh.shape["occ"], mesh.shape["rep"]),
        mesh=mesh, in_specs=in_specs, out_specs=P(both, None), check_vma=False,
    )
```

```python
import functools

import jax
import jax.numpy as jnp
from jax import lax
from jax.experimental import pallas as pl
from jax.experimental.pallas import tpu as pltpu
from jax.sharding import PartitionSpec as P

MESH = pl.DeviceIdType.MESH
NBLK = 32
KN = 2
BF = jnp.bfloat16
F32 = jnp.float32
NT = (((1,), (1,)), ((), ()))


def split(x):
    hi = x.astype(BF)
    return hi, (x - hi.astype(F32)).astype(BF)


def mm(a, b):
    return jnp.dot(a, b, preferred_element_type=F32)


def mm_nt(a, b):
    return lax.dot_general(a, b, NT, preferred_element_type=F32)


def kernel(
    n_occ, n_rep, n, domb, npno, blk, nx, nz,
    cnt, fown, fpair, coef, coefs, amp, den, near, dom,
    out,
    G0, G1, G2, G3, F, PS, RA, RZ, SF, T0, TP, GP, GT, RT, ST, FT, RR, RQ, rqs, DT, IV, ivs, acc, BD, W,
    BKs, BKr, BS, BB, X,
    ysend, yrecv, tsend, trecv, p1s, p1r, p2s, p2r, bs, br, lsem,
):
    me = lax.axis_index("occ")
    rep = lax.axis_index("rep")
    cores = n_occ // (nx * nz)
    mx, mz, mc = me // (nz * cores), lax.rem(me // cores, nz), lax.rem(me, cores)
    req = n * KN
    group = n * n_rep
    tiles = npno * npno // 128
    per = domb * npno // 8 // n_occ
    lane = lax.broadcasted_iota(jnp.int32, (8, 128), 1)
    sub = lax.broadcasted_iota(jnp.int32, (8, 128), 0)
    low = lane < npno
    G = (G0, G1, G2, G3)

    def occ_dev(d):
        return {"occ": d}

    def rep_dev(r):
        return {"rep": lax.rem(rep + r, n_rep)}

    def at(dx, dz, dc):
        return (lax.rem(mx + dx, nx) * nz + lax.rem(mz + dz, nz)) * cores + lax.rem(mc + dc, cores)

    def peer(k):
        dx, rest = lax.rem(k, nx), k // nx
        return at(dx, lax.rem(rest + dx, nz), rest // nz)

    def span(d, m):
        return min(d, m - d)

    outward = sorted(
        [(dx, dz, dc) for dc in range(cores) for dz in range(nz) for dx in range(nx) if (dx, dz, dc) != (0, 0, 0)],
        key=lambda o: -(span(o[0], nx) + span(o[1], nz)))

    barrier = pltpu.get_barrier_semaphore()
    for o in outward:
        pl.semaphore_signal(barrier, inc=1, device_id=occ_dev(at(*o)), device_id_type=MESH)
    for r in range(1, n_rep):
        pl.semaphore_signal(barrier, inc=1, device_id=rep_dev(r), device_id_type=MESH)

    blocks = pl.ds(0, domb)
    own = pltpu.make_async_copy(coef, G0.at[:, blocks], lsem.at[0])
    own.start()
    cuts = [
        pltpu.make_async_copy(coefs.at[p, t], PS.at[:, n * t + p], lsem.at[4 + per * p + t])
        for p in range(n) for t in range(per)]
    for c in cuts:
        c.start()

    rr = jnp.zeros((1, 128), jnp.int32)
    lane1 = lax.broadcasted_iota(jnp.int32, (1, 128), 1)
    base = lax.rem(me * req, 128)
    for j in range(req):
        rr = jnp.where(lane1 == base + j, fown[j % KN, j // KN] * 8 + fpair[j % KN, j // KN], rr)
    RR[...] = rr
    RQ[me] = rr

    cntv = jnp.zeros((8, 128), jnp.int32)
    for p in range(n):
        cntv = jnp.where(sub == p, cnt[p], cntv)
    col = lax.rem(lane, npno)
    up = lane // npno
    pad = jnp.zeros((8 - n, 128), F32)
    last = None
    for i in range(tiles):
        x = jnp.concatenate([amp[:, 128 * i : 128 * i + 128].astype(F32), pad], axis=0)
        live = (2 * i + up < cntv) & (col < cntv)
        x = jnp.where(live, x, 0.0)
        T0[pl.ds(8 * i, 8), :] = x
        PS[i, n * per] = x.astype(BF)
        if i % 2:
            TP[i // 2] = (last + pltpu.roll(x, n, 0)).astype(BF)
        last = x

    dt = jnp.concatenate([dom[...], jnp.zeros((-domb % 8, dom.shape[1]), jnp.int32)], axis=0)
    DT[...] = dt.T
    rows_d = [DT[pl.ds(pl.multiple_of(me * group, group), group), :]]
    for j in range(req):
        owner, pair = fown[j % KN, j // KN], fpair[j % KN, j // KN]
        rows_d.append(DT[pl.ds((owner * n_rep + rep) * n + pair, 1), :])
    dd = jnp.concatenate(rows_d, axis=0)
    lane_i = lax.broadcasted_iota(jnp.int32, (group + req, 128), 1)
    inv = jnp.full((group + req, 128), domb, jnp.int32)
    for a in range(domb):
        inv = jnp.where(dd[:, a : a + 1] == lane_i, a, inv)
    IV[pl.ds(0, group), :] = inv[:group]
    fi = inv[group:]
    have = fi < domb
    IV[pl.ds(group, req), :] = jnp.where(have, lax.rem(fi * 8, n_occ), n_occ)
    IV[pl.ds(group + req, req), :] = jnp.where(have, (fi * 8) // n_occ, 0)
    IV[pl.ds(group + 2 * req, group), pl.ds(0, dd.shape[1])] = dd[:group]

    for g in G:
        g[:, domb] = jnp.zeros((n, npno, blk), BF)
    for j in range(req):
        F[pl.ds(n_occ, 8), j] = jnp.zeros((8, 8, blk), BF)
    for c in cuts:
        c.wait()
    RA[me] = PS[me, pl.ds(0, n)]
    RZ[me] = PS[me, pl.ds(n, n * (per - 1) + 1)]

    pl.semaphore_wait(barrier, n_occ - 1 + n_rep - 1)
    index = pltpu.make_async_copy(IV, ivs, lsem.at[3])
    index.start()

    half = n // 2
    ahead, behind = 1, n_rep - 1
    opposite = n_rep // 2

    def halfway(src, h, to, r, s):
        return pltpu.make_async_remote_copy(
            src, G[to].at[pl.ds(h * half, half), blocks], ysend.at[s], yrecv.at[s],
            device_id=rep_dev(r), device_id_type=MESH)

    firsts = [
        halfway(coef.at[pl.ds(0, half)], 0, behind, ahead, 0),
        halfway(coef.at[pl.ds(half, half)], 1, ahead, behind, 1),
        halfway(coef.at[pl.ds(half, half)], 1, behind, ahead, 2),
        halfway(coef.at[pl.ds(0, half)], 0, ahead, behind, 3)]
    relays = [
        halfway(G[behind].at[pl.ds(0, half), blocks], 0, opposite, ahead, 4),
        halfway(G[ahead].at[pl.ds(half, half), blocks], 1, opposite, behind, 5)]
    firsts[0].start()
    firsts[1].start()
    amps = []
    for r in range(1, n_rep):
        t = pltpu.make_async_remote_copy(
            TP, GP.at[n_rep - r], tsend.at[r], trecv.at[n_rep - r], device_id=rep_dev(r), device_id_type=MESH)
        t.start()
        amps.append(t)
    firsts[2].start()
    firsts[3].start()

    def slices(o, piece):
        d = at(*o)
        part, to = (pl.ds(n, n * (per - 1) + 1), RZ) if piece else (pl.ds(0, n), RA)
        pltpu.make_async_remote_copy(
            PS.at[d, part], to.at[me], p1s.at[1 + piece], p1r.at[1 + piece],
            device_id=occ_dev(d), device_id_type=MESH).start()

    for o in outward[:8]:
        slices(o, 0)
    for o in outward:
        pltpu.make_async_remote_copy(
            RR, RQ.at[me], p1s.at[0], p1r.at[0], device_id=occ_dev(at(*o)), device_id_type=MESH).start()
    for o in outward[8:]:
        slices(o, 0)
    for o in outward:
        slices(o, 1)

    def wait_all(ref, sem):
        pltpu.make_async_copy(ref, ref, sem).wait()

    index.wait()
    own.wait()
    GP[0] = TP[...]
    lane32 = lax.broadcasted_iota(jnp.int32, (npno // 2, 128), 1) < npno
    low64 = lax.broadcasted_iota(jnp.int32, (npno, 128), 1) < npno

    def place(x, slot, odd):
        other = pltpu.roll(x, npno, 1)
        if odd:
            BD[slot, pl.ds(npno, npno // 2, stride=2), :] = jnp.where(lane32, 0.0, other)
            BD[slot, pl.ds(npno + 1, npno // 2, stride=2), :] = jnp.where(lane32, 0.0, x)
        else:
            BD[slot, pl.ds(0, npno // 2, stride=2), :] = jnp.where(lane32, x, 0.0)
            BD[slot, pl.ds(1, npno // 2, stride=2), :] = jnp.where(lane32, other, 0.0)

    def near_part(r, gains):
        dev = lax.rem(rep + r, n_rep)
        acc[...] = jnp.zeros_like(acc)

        def overlap(b, c):
            hs, gs = [], []
            for t in range(4):
                bb = 4 * b + t
                hs.append(jnp.concatenate([G0[p, ivs[rep * n + p, bb]] for p in range(n)], axis=0))
                gs.append(jnp.concatenate([G[r][q, ivs[dev * n + q, bb]] for q in range(n)], axis=0))
            acc[...] += mm_nt(jnp.concatenate(hs, axis=1), jnp.concatenate(gs, axis=1))
            return c

        lax.fori_loop(0, NBLK // 4, overlap, 0)
        GT[...] = GP[r].astype(F32).reshape(n * tiles, 128)
        for q in range(n):
            place(GT[pl.ds(q, npno // 2, stride=n), :], (n * r + q) // 2, q % 2)
        parts = [[] for _ in range(n)]
        for k in range(n // 2):
            hi, lo = split(acc[:, 128 * k : 128 * k + 128])
            bd = BD[n // 2 * r + k].astype(BF)
            u = mm(jnp.concatenate([hi, lo], axis=1), jnp.concatenate([bd, bd], axis=0))
            q = dev * n + 2 * k
            c0 = jnp.sum((near[...] == q).astype(F32), axis=1, keepdims=True)
            c1 = jnp.sum((near[...] == q + 1).astype(F32), axis=1, keepdims=True)
            w = jnp.where(low[:n], c0, c1)
            for p in range(n):
                rows = slice(p * npno, (p + 1) * npno)
                uh, ul = split(u[rows] * w[p : p + 1])
                parts[p].append((uh, ul, hi[rows], lo[rows]))
        for p in range(n):
            uh, ul, sh, sl = (jnp.concatenate(v, axis=1) for v in zip(*parts[p]))
            g = mm_nt(uh, sh) + mm_nt(ul, sh) + mm_nt(uh, sl)
            if gains:
                g = g + W[2 * req + p, :, pl.ds(0, npno)]
            W[2 * req + p, :, pl.ds(0, npno)] = g

    near_part(0, False)

    wait_all(RQ.at[pl.ds(0, n_occ - 1)], p1r.at[0])
    table = pltpu.make_async_copy(RQ, rqs, lsem.at[2])
    table.start()
    table.wait()
    others = pl.ds(0, n_occ - 1)
    cut = (pl.ds(0, req), pl.ds(req, req * (per - 1) + 1))

    def gather(d, dst, piece):
        for j in range(req):
            r = rqs[d, 0, lax.rem(d * req + j, 128)]
            src, pair = r >> 3, r & 7
            if piece:
                for t in range(per - 1):
                    dst[d, req * (t + 1) + j] = RZ[src, n * t + pair]
                ST[pl.ds(8 * d + j, 1), :] = RT[pl.ds(r, 1), :]
            else:
                dst[d, j] = RA[src, pair]
        if piece:
            dst[d, req * per] = ST[pl.ds(8 * d, 8), :].astype(BF)

    def ship(d, piece):
        pltpu.make_async_remote_copy(
            SF.at[d, cut[piece]], F.at[me, cut[piece]], p2s.at[piece], p2r.at[piece],
            device_id=occ_dev(d), device_id_type=MESH).start()

    def answer_all(piece):
        gather(peer(1), SF, piece)

        def answer(k, c):
            gather(peer(k), SF, piece)
            ship(peer(k - 1), piece)
            return c

        lax.fori_loop(2, n_occ, answer, 0)
        ship(peer(n_occ - 1), piece)

    wait_all(RA.at[others], p1r.at[1])
    answer_all(0)
    for t in range(2):
        firsts[t].wait_recv()
        relays[t].start()
    wait_all(RZ.at[others], p1r.at[2])
    RT[...] = RZ[:, n * (per - 1)].astype(F32).reshape(8 * n_occ, 128)
    answer_all(1)
    gather(me, F, 0)
    gather(me, F, 1)

    for t in amps:
        t.wait_recv()
    firsts[3].wait_recv()
    near_part(ahead, True)
    firsts[2].wait_recv()
    near_part(behind, True)

    for t in range(2):
        wait_all(F.at[others, cut[t]], p2r.at[t])
    FT[...] = F[pl.ds(0, n_occ), req * per].astype(F32).reshape(8 * n_occ, 128)
    for j in range(req):
        place(FT[pl.ds(j, npno // 2, stride=8), :], (group + j) // 2, j % 2)

    def flat(slot):
        e = W[slot, pl.ds(0, npno // 2, stride=2), :]
        o = W[slot, pl.ds(1, npno // 2, stride=2), :]
        return jnp.where(lane32, e, pltpu.roll(o, npno, 1))

    def block(j, p, a):
        b = ivs[group + 2 * req + rep * n + p, a]
        return F[pl.ds(ivs[group + j, b], 8), req * ivs[group + req + j, b] + j].reshape(npno, blk)

    z = jnp.zeros((npno, 128), BF)
    for p in range(n):
        h = jnp.concatenate([G0[p, a] for a in range(domb)], axis=1)
        f = jnp.concatenate([
            jnp.concatenate([block(j, p, a) for a in range(domb)], axis=1)
            for j in range(KN * p, KN * p + KN)], axis=0)
        s = mm_nt(h, f)
        sh, sl = split(s)
        th, tl = split(s.T)
        bd = BD[group // 2 + p].astype(BF)
        u = mm(jnp.concatenate([sh, sl], axis=1), jnp.concatenate([bd, bd], axis=0))
        odd = p % 2
        tp = BD[p // 2, pl.ds(odd * npno, npno), :].astype(BF)
        v = mm(jnp.concatenate([tp, tp], axis=1),
               jnp.concatenate([z, sh, z, sl] if odd else [sh, z, sl, z], axis=0))
        vh, vl = split(v)
        b = mm(th, vh) + mm(tl, vh) + mm(th, vl)
        W[KN * p, :, :] = b[:npno]
        W[KN * p + 1, :, :] = pltpu.roll(b[npno:], npno, 1)
        uh, ul = split(u)
        W[2 * req + p, :, pl.ds(0, npno)] += mm_nt(uh, sh) + mm_nt(ul, sh) + mm_nt(uh, sl)
    for j in range(req):
        BKs[pl.ds(j, npno // 2, stride=8), :] = flat(j)

    def back(src, dst, s):
        for o in outward:
            d = at(*o)
            pltpu.make_async_remote_copy(
                src.at[pl.ds(8 * d, 8)], dst.at[pl.ds(8 * me, 8)], bs.at[s], br.at[s],
                device_id=occ_dev(d), device_id_type=MESH).start()
        dst[pl.ds(8 * me, 8), :] = src[pl.ds(8 * me, 8), :]

    rows_in = pl.ds(0, 8 * (n_occ - 1))
    back(BKs, BKr, 0)
    for t in relays:
        t.wait_recv()
    near_part(opposite, True)
    hn = n_occ // 2
    ids = jnp.concatenate(
        [jnp.sum(RQ[pl.ds(h * hn, hn)], axis=0) for h in range(2)], axis=1)
    hot = (lax.broadcasted_iota(jnp.int32, (8 * n_occ, req * n_occ), 0) == ids).astype(F32).astype(BF)
    for p in range(n):
        X[pl.ds(p, npno // 2, stride=8), :] = flat(2 * req + p)
    de = jnp.concatenate([den[...], jnp.zeros((8 - n, npno), F32)], axis=0)
    db = jnp.concatenate([de, de], axis=1)
    for i in range(tiles):
        r = pl.ds(8 * i, 8)
        da = jnp.where(low, de[:, 2 * i : 2 * i + 1], de[:, 2 * i + 1 : 2 * i + 2])
        X[r, :] = (da + db) * T0[r, :] + X[r, :]
    wait_all(BKr.at[rows_in], br.at[0])
    kh, kl = split(BKr[...])
    BS[...] = mm(hot, kh) + mm(hot, kl)
    back(BS, BB, 1)
    wait_all(BB.at[rows_in], br.at[1])
    for i in range(tiles):
        r = pl.ds(8 * i, 8)
        live = (2 * i + up < cntv) & (col < cntv)
        out[:, 128 * i : 128 * i + 128] = jnp.where(live, X[r, :] + BB[r, :], 0.0)[:n]

    for c in firsts + relays + amps:
        c.wait_send()
    wait_all(RQ.at[pl.ds(0, n_occ - 1)], p1s.at[0])
    wait_all(RA.at[others], p1s.at[1])
    wait_all(RZ.at[others], p1s.at[2])
    for t in range(2):
        wait_all(F.at[others, cut[t]], p2s.at[t])
    wait_all(BKr.at[rows_in], bs.at[0])
    wait_all(BB.at[rows_in], bs.at[1])


def on_device(n_occ, n_rep, coeffs, amplitudes, denominators, pno_count, domains, far_owner, far_pair, near_pair):
    n, domb, npno, blk = coeffs.shape
    group = n * n_rep
    req = n * KN
    i32 = jnp.int32
    smem = pl.BlockSpec(memory_space=pltpu.SMEM)
    vmem = pl.BlockSpec(memory_space=pltpu.VMEM)
    anym = pl.BlockSpec(memory_space=pl.ANY)
    rows = 8 * n_occ
    per = domb * npno // 8 // n_occ
    tiles = npno * npno // 128
    V = pltpu.VMEM
    dma = pltpu.SemaphoreType.DMA
    return pl.pallas_call(
        functools.partial(kernel, n_occ, n_rep, n, domb, npno, blk, 4, 4),
        out_shape=jax.ShapeDtypeStruct((n, npno * npno), F32),
        in_specs=[smem] * 3 + [anym, anym] + [vmem] * 4,
        out_specs=vmem,
        scratch_shapes=[V((n, domb + 1, npno, blk), BF)] * 4 + [
            V((n_occ + 8, req * per + 1, 8, blk), BF),
            V((n_occ, n * per + 1, 8, blk), BF),
            V((n_occ, n, 8, blk), BF),
            V((n_occ, n * (per - 1) + 1, 8, blk), BF),
            V((n_occ, req * per + 1, 8, blk), BF),
            V((rows, 128), F32),
            V((tiles // 2, 8, 128), BF),
            V((n_rep, tiles // 2, 8, 128), BF),
            V((n * tiles, 128), F32),
            V((rows, 128), F32),
            V((rows, 128), F32),
            V((rows, 128), F32),
            V((1, 128), i32),
            V((n_occ, 1, 128), i32),
            pltpu.SMEM((n_occ, 1, 128), i32),
            V((domains.shape[0], domb + -domb % 8), i32),
            V((2 * group + 2 * req, 128), i32),
            pltpu.SMEM((2 * group + 2 * req, 128), i32),
            V((n * npno, n * npno), F32),
            V((group // 2 + n, 128, 128), F32),
            V((2 * req + n, npno, 128), F32),
            V((rows, 128), F32),
            V((rows, 128), F32),
            V((rows, 128), F32),
            V((rows, 128), F32),
            V((rows, 128), F32),
            dma((6,)), dma((6,)), dma((n_rep,)), dma((n_rep,)),
            dma((3,)), dma((3,)), dma((2,)), dma((2,)), dma((2,)), dma((2,)), dma((4 + n * per,)),
        ],
        compiler_params=pltpu.CompilerParams(
            collective_id=0, has_side_effects=True, vmem_limit_bytes=56 * 1024 * 1024),
    )(pno_count, far_owner.T, far_pair.T, coeffs, coeffs.reshape(n, per, n_occ, 8, blk),
      amplitudes, denominators, near_pair, domains.T)


def solution(mesh):
    both = ("occ", "rep")
    in_specs = (
        P(both, None, None, None), P(both, None), P(both, None), P(both),
        P(), P(both, None), P(both, None), P(both, None),
    )
    return jax.shard_map(
        functools.partial(on_device, mesh.shape["occ"], mesh.shape["rep"]),
        mesh=mesh, in_specs=in_specs, out_specs=P(both, None), check_vma=False,
    )
```

```python
import functools

import jax
import jax.numpy as jnp
from jax import lax
from jax.experimental import pallas as pl
from jax.experimental.pallas import tpu as pltpu
from jax.sharding import PartitionSpec as P

MESH = pl.DeviceIdType.MESH
NBLK = 32
KN = 2
BF = jnp.bfloat16
F32 = jnp.float32
NT = (((1,), (1,)), ((), ()))


def split(x):
    hi = x.astype(BF)
    return hi, (x - hi.astype(F32)).astype(BF)


def mm(a, b):
    return jnp.dot(a, b, preferred_element_type=F32)


def mm_nt(a, b):
    return lax.dot_general(a, b, NT, preferred_element_type=F32)


def kernel(
    n_occ, n_rep, n, domb, npno, blk, nx, nz,
    cnt, fown, fpair, coef, coefs, amp, den, near, dom,
    out,
    G0, G1, G2, G3, F, PS, RA, RZ, SF, T0, TP, GP, GT, RT, ST, FT, RR, RQ, rqs, DT, IV, ivs, FI, acc, BD, W,
    BKs, BKr, BS, BB, X,
    ysend, yrecv, tsend, trecv, p1s, p1r, p2s, p2r, bs, br, lsem,
):
    me = lax.axis_index("occ")
    rep = lax.axis_index("rep")
    cores = n_occ // (nx * nz)
    mx, mz, mc = me // (nz * cores), lax.rem(me // cores, nz), lax.rem(me, cores)
    req = n * KN
    group = n * n_rep
    tiles = npno * npno // 128
    per = domb * npno // 8 // n_occ
    lane = lax.broadcasted_iota(jnp.int32, (8, 128), 1)
    sub = lax.broadcasted_iota(jnp.int32, (8, 128), 0)
    low = lane < npno
    G = (G0, G1, G2, G3)

    def occ_dev(d):
        return {"occ": d}

    def rep_dev(r):
        return {"rep": lax.rem(rep + r, n_rep)}

    def at(dx, dz, dc):
        return (lax.rem(mx + dx, nx) * nz + lax.rem(mz + dz, nz)) * cores + lax.rem(mc + dc, cores)

    def span(d, m):
        return min(d, m - d)

    outward = sorted(
        [(dx, dz, dc) for dc in range(cores) for dz in range(nz) for dx in range(nx) if (dx, dz, dc) != (0, 0, 0)],
        key=lambda o: -(span(o[0], nx) + span(o[1], nz)))

    barrier = pltpu.get_barrier_semaphore()
    for o in outward:
        pl.semaphore_signal(barrier, inc=1, device_id=occ_dev(at(*o)), device_id_type=MESH)
    for r in range(1, n_rep):
        pl.semaphore_signal(barrier, inc=1, device_id=rep_dev(r), device_id_type=MESH)

    blocks = pl.ds(0, domb)
    own = pltpu.make_async_copy(coef, G0.at[:, blocks], lsem.at[0])
    own.start()
    cuts = [
        pltpu.make_async_copy(coefs.at[p, t], PS.at[:, n * t + p], lsem.at[4 + per * p + t])
        for p in range(n) for t in range(per)]
    for c in cuts:
        c.start()

    rr = jnp.zeros((1, 128), jnp.int32)
    lane1 = lax.broadcasted_iota(jnp.int32, (1, 128), 1)
    base = lax.rem(me * req, 128)
    for j in range(req):
        rr = jnp.where(lane1 == base + j, fown[j % KN, j // KN] * 8 + fpair[j % KN, j // KN], rr)
    RR[...] = rr
    RQ[me] = rr

    cntv = jnp.zeros((8, 128), jnp.int32)
    for p in range(n):
        cntv = jnp.where(sub == p, cnt[p], cntv)
    col = lax.rem(lane, npno)
    up = lane // npno
    pad = jnp.zeros((8 - n, 128), F32)
    last = None
    for i in range(tiles):
        x = jnp.concatenate([amp[:, 128 * i : 128 * i + 128].astype(F32), pad], axis=0)
        live = (2 * i + up < cntv) & (col < cntv)
        x = jnp.where(live, x, 0.0)
        T0[pl.ds(8 * i, 8), :] = x
        PS[i, n * per] = x.astype(BF)
        if i % 2:
            TP[i // 2] = (last + pltpu.roll(x, n, 0)).astype(BF)
        last = x

    dt = jnp.concatenate([dom[...], jnp.zeros((-domb % 8, dom.shape[1]), jnp.int32)], axis=0)
    DT[...] = dt.T
    rows_d = [DT[pl.ds(pl.multiple_of(me * group, group), group), :]]
    for j in range(req):
        owner, pair = fown[j % KN, j // KN], fpair[j % KN, j // KN]
        rows_d.append(DT[pl.ds((owner * n_rep + rep) * n + pair, 1), :])
    dd = jnp.concatenate(rows_d, axis=0)
    lane_i = lax.broadcasted_iota(jnp.int32, (group + req, 128), 1)
    inv = jnp.full((group + req, 128), domb, jnp.int32)
    for a in range(domb):
        inv = jnp.where(dd[:, a : a + 1] == lane_i, a, inv)
    IV[pl.ds(0, group), :] = inv[:group]
    fi = inv[group:]
    have = fi < domb
    IV[pl.ds(group, req), :] = jnp.where(have, lax.rem(fi * 8, n_occ), n_occ)
    IV[pl.ds(group + req, req), :] = jnp.where(have, (fi * 8) // n_occ, 0)
    IV[pl.ds(group + 2 * req, group), pl.ds(0, dd.shape[1])] = dd[:group]

    for g in G:
        g[:, domb] = jnp.zeros((n, npno, blk), BF)
    for j in range(req):
        F[pl.ds(n_occ, 8), j] = jnp.zeros((8, 8, blk), BF)
    for c in cuts:
        c.wait()
    RA[me] = PS[me, pl.ds(0, n)]
    RZ[me] = PS[me, pl.ds(n, n * (per - 1) + 1)]

    pl.semaphore_wait(barrier, n_occ - 1 + n_rep - 1)
    index = pltpu.make_async_copy(IV, ivs, lsem.at[3])
    index.start()

    half = n // 2
    ahead, behind = 1, n_rep - 1
    opposite = n_rep // 2

    def halfway(src, h, to, r, s):
        return pltpu.make_async_remote_copy(
            src, G[to].at[pl.ds(h * half, half), blocks], ysend.at[s], yrecv.at[s],
            device_id=rep_dev(r), device_id_type=MESH)

    firsts = [
        halfway(coef.at[pl.ds(0, half)], 0, behind, ahead, 0),
        halfway(coef.at[pl.ds(half, half)], 1, ahead, behind, 1),
        halfway(coef.at[pl.ds(half, half)], 1, behind, ahead, 2),
        halfway(coef.at[pl.ds(0, half)], 0, ahead, behind, 3)]
    relays = [
        halfway(G[behind].at[pl.ds(0, half), blocks], 0, opposite, ahead, 4),
        halfway(G[ahead].at[pl.ds(half, half), blocks], 1, opposite, behind, 5)]
    firsts[0].start()
    firsts[1].start()
    amps = []
    for r in range(1, n_rep):
        t = pltpu.make_async_remote_copy(
            TP, GP.at[n_rep - r], tsend.at[r], trecv.at[n_rep - r], device_id=rep_dev(r), device_id_type=MESH)
        t.start()
        amps.append(t)
    firsts[2].start()
    firsts[3].start()

    def slices(o, piece):
        d = at(*o)
        part, to = (pl.ds(n, n * (per - 1) + 1), RZ) if piece else (pl.ds(0, n), RA)
        pltpu.make_async_remote_copy(
            PS.at[d, part], to.at[me], p1s.at[1 + piece], p1r.at[1 + piece],
            device_id=occ_dev(d), device_id_type=MESH).start()

    for o in outward[:8]:
        slices(o, 0)
    for o in outward:
        pltpu.make_async_remote_copy(
            RR, RQ.at[me], p1s.at[0], p1r.at[0], device_id=occ_dev(at(*o)), device_id_type=MESH).start()
    for o in outward[8:]:
        slices(o, 0)
    for o in outward:
        slices(o, 1)

    def wait_all(ref, sem):
        pltpu.make_async_copy(ref, ref, sem).wait()

    index.wait()
    own.wait()
    GP[0] = TP[...]
    lane32 = lax.broadcasted_iota(jnp.int32, (npno // 2, 128), 1) < npno
    low64 = lax.broadcasted_iota(jnp.int32, (npno, 128), 1) < npno

    def place(x, slot, odd):
        other = pltpu.roll(x, npno, 1)
        if odd:
            BD[slot, pl.ds(npno, npno // 2, stride=2), :] = jnp.where(lane32, 0.0, other)
            BD[slot, pl.ds(npno + 1, npno // 2, stride=2), :] = jnp.where(lane32, 0.0, x)
        else:
            BD[slot, pl.ds(0, npno // 2, stride=2), :] = jnp.where(lane32, x, 0.0)
            BD[slot, pl.ds(1, npno // 2, stride=2), :] = jnp.where(lane32, other, 0.0)

    def near_part(r, gains):
        dev = lax.rem(rep + r, n_rep)
        acc[...] = jnp.zeros_like(acc)

        def overlap(b, c):
            hs, gs = [], []
            for t in range(4):
                bb = 4 * b + t
                hs.append(jnp.concatenate([G0[p, ivs[rep * n + p, bb]] for p in range(n)], axis=0))
                gs.append(jnp.concatenate([G[r][q, ivs[dev * n + q, bb]] for q in range(n)], axis=0))
            acc[...] += mm_nt(jnp.concatenate(hs, axis=1), jnp.concatenate(gs, axis=1))
            return c

        lax.fori_loop(0, NBLK // 4, overlap, 0)
        GT[...] = GP[r].astype(F32).reshape(n * tiles, 128)
        for q in range(n):
            place(GT[pl.ds(q, npno // 2, stride=n), :], (n * r + q) // 2, q % 2)
        parts = [[] for _ in range(n)]
        for k in range(n // 2):
            hi, lo = split(acc[:, 128 * k : 128 * k + 128])
            bd = BD[n // 2 * r + k].astype(BF)
            u = mm(jnp.concatenate([hi, lo], axis=1), jnp.concatenate([bd, bd], axis=0))
            q = dev * n + 2 * k
            c0 = jnp.sum((near[...] == q).astype(F32), axis=1, keepdims=True)
            c1 = jnp.sum((near[...] == q + 1).astype(F32), axis=1, keepdims=True)
            w = jnp.where(low[:n], c0, c1)
            for p in range(n):
                rows = slice(p * npno, (p + 1) * npno)
                uh, ul = split(u[rows] * w[p : p + 1])
                parts[p].append((uh, ul, hi[rows], lo[rows]))
        for p in range(n):
            uh, ul, sh, sl = (jnp.concatenate(v, axis=1) for v in zip(*parts[p]))
            g = mm_nt(uh, sh) + mm_nt(ul, sh) + mm_nt(uh, sl)
            if gains:
                g = g + W[2 * req + p, :, pl.ds(0, npno)]
            W[2 * req + p, :, pl.ds(0, npno)] = g

    near_part(0, False)

    wait_all(RQ.at[pl.ds(0, n_occ - 1)], p1r.at[0])
    table = pltpu.make_async_copy(RQ, rqs, lsem.at[2])
    table.start()
    table.wait()
    others = pl.ds(0, n_occ - 1)
    cut = (pl.ds(0, req), pl.ds(req, req * (per - 1) + 1))

    def gather(d, dst, piece):
        for j in range(req):
            r = rqs[d, 0, lax.rem(d * req + j, 128)]
            src, pair = r >> 3, r & 7
            if piece:
                for t in range(per - 1):
                    dst[d, req * (t + 1) + j] = RZ[src, n * t + pair]
                ST[pl.ds(8 * d + j, 1), :] = RT[pl.ds(r, 1), :]
            else:
                dst[d, j] = RA[src, pair]
        if piece:
            dst[d, req * per] = ST[pl.ds(8 * d, 8), :].astype(BF)

    def ship(d, piece):
        pltpu.make_async_remote_copy(
            SF.at[d, cut[piece]], F.at[me, cut[piece]], p2s.at[piece], p2r.at[piece],
            device_id=occ_dev(d), device_id_type=MESH).start()

    def answer_all(piece):
        last = None
        for o in outward:
            d = at(*o)
            gather(d, SF, piece)
            if last is not None:
                ship(last, piece)
            last = d
        ship(last, piece)

    wait_all(RA.at[others], p1r.at[1])
    answer_all(0)
    for t in range(2):
        firsts[t].wait_recv()
        relays[t].start()
    wait_all(RZ.at[others], p1r.at[2])
    RT[...] = RZ[:, n * (per - 1)].astype(F32).reshape(8 * n_occ, 128)
    answer_all(1)
    gather(me, F, 0)
    gather(me, F, 1)

    for t in amps:
        t.wait_recv()
    firsts[3].wait_recv()
    near_part(ahead, True)
    firsts[2].wait_recv()
    near_part(behind, True)

    for j in range(req):
        for a in range(domb):
            b = ivs[group + 2 * req + rep * n + j // KN, a]
            FI[2 * (j * domb + a)] = ivs[group + j, b]
            FI[2 * (j * domb + a) + 1] = req * ivs[group + req + j, b] + j
    for t in range(2):
        wait_all(F.at[others, cut[t]], p2r.at[t])
    FT[...] = F[pl.ds(0, n_occ), req * per].astype(F32).reshape(8 * n_occ, 128)
    for j in range(req):
        place(FT[pl.ds(j, npno // 2, stride=8), :], (group + j) // 2, j % 2)

    def flat(slot):
        e = W[slot, pl.ds(0, npno // 2, stride=2), :]
        o = W[slot, pl.ds(1, npno // 2, stride=2), :]
        return jnp.where(lane32, e, pltpu.roll(o, npno, 1))

    def block(j, a):
        at_ja = 2 * (j * domb + a)
        return F[pl.ds(FI[at_ja], 8), FI[at_ja + 1]].reshape(npno, blk)

    z = jnp.zeros((npno, 128), BF)
    for p in range(n):
        h = jnp.concatenate([G0[p, a] for a in range(domb)], axis=1)
        f = jnp.concatenate([
            jnp.concatenate([block(j, a) for a in range(domb)], axis=1)
            for j in range(KN * p, KN * p + KN)], axis=0)
        s = mm_nt(h, f)
        sh, sl = split(s)
        th, tl = split(s.T)
        bd = BD[group // 2 + p].astype(BF)
        u = mm(jnp.concatenate([sh, sl], axis=1), jnp.concatenate([bd, bd], axis=0))
        odd = p % 2
        tp = BD[p // 2, pl.ds(odd * npno, npno), :].astype(BF)
        v = mm(jnp.concatenate([tp, tp], axis=1),
               jnp.concatenate([z, sh, z, sl] if odd else [sh, z, sl, z], axis=0))
        vh, vl = split(v)
        b = mm(th, vh) + mm(tl, vh) + mm(th, vl)
        W[KN * p, :, :] = b[:npno]
        W[KN * p + 1, :, :] = pltpu.roll(b[npno:], npno, 1)
        uh, ul = split(u)
        W[2 * req + p, :, pl.ds(0, npno)] += mm_nt(uh, sh) + mm_nt(ul, sh) + mm_nt(uh, sl)
    for j in range(req):
        BKs[pl.ds(j, npno // 2, stride=8), :] = flat(j)

    def back(src, dst, s):
        for o in outward:
            d = at(*o)
            pltpu.make_async_remote_copy(
                src.at[pl.ds(8 * d, 8)], dst.at[pl.ds(8 * me, 8)], bs.at[s], br.at[s],
                device_id=occ_dev(d), device_id_type=MESH).start()
        dst[pl.ds(8 * me, 8), :] = src[pl.ds(8 * me, 8), :]

    rows_in = pl.ds(0, 8 * (n_occ - 1))
    back(BKs, BKr, 0)
    for t in relays:
        t.wait_recv()
    near_part(opposite, True)
    hn = n_occ // 2
    ids = jnp.concatenate(
        [jnp.sum(RQ[pl.ds(h * hn, hn)], axis=0) for h in range(2)], axis=1)
    hot = (lax.broadcasted_iota(jnp.int32, (8 * n_occ, req * n_occ), 0) == ids).astype(F32).astype(BF)
    for p in range(n):
        X[pl.ds(p, npno // 2, stride=8), :] = flat(2 * req + p)
    de = jnp.concatenate([den[...], jnp.zeros((8 - n, npno), F32)], axis=0)
    db = jnp.concatenate([de, de], axis=1)
    for i in range(tiles):
        r = pl.ds(8 * i, 8)
        da = jnp.where(low, de[:, 2 * i : 2 * i + 1], de[:, 2 * i + 1 : 2 * i + 2])
        X[r, :] = (da + db) * T0[r, :] + X[r, :]
    wait_all(BKr.at[rows_in], br.at[0])
    kh, kl = split(BKr[...])
    BS[...] = mm(hot, kh) + mm(hot, kl)
    back(BS, BB, 1)
    wait_all(BB.at[rows_in], br.at[1])
    for i in range(tiles):
        r = pl.ds(8 * i, 8)
        live = (2 * i + up < cntv) & (col < cntv)
        out[:, 128 * i : 128 * i + 128] = jnp.where(live, X[r, :] + BB[r, :], 0.0)[:n]

    for c in firsts + relays + amps:
        c.wait_send()
    wait_all(RQ.at[pl.ds(0, n_occ - 1)], p1s.at[0])
    wait_all(RA.at[others], p1s.at[1])
    wait_all(RZ.at[others], p1s.at[2])
    for t in range(2):
        wait_all(F.at[others, cut[t]], p2s.at[t])
    wait_all(BKr.at[rows_in], bs.at[0])
    wait_all(BB.at[rows_in], bs.at[1])


def on_device(n_occ, n_rep, coeffs, amplitudes, denominators, pno_count, domains, far_owner, far_pair, near_pair):
    n, domb, npno, blk = coeffs.shape
    group = n * n_rep
    req = n * KN
    i32 = jnp.int32
    smem = pl.BlockSpec(memory_space=pltpu.SMEM)
    vmem = pl.BlockSpec(memory_space=pltpu.VMEM)
    anym = pl.BlockSpec(memory_space=pl.ANY)
    rows = 8 * n_occ
    per = domb * npno // 8 // n_occ
    tiles = npno * npno // 128
    V = pltpu.VMEM
    dma = pltpu.SemaphoreType.DMA
    return pl.pallas_call(
        functools.partial(kernel, n_occ, n_rep, n, domb, npno, blk, 4, 4),
        out_shape=jax.ShapeDtypeStruct((n, npno * npno), F32),
        in_specs=[smem] * 3 + [anym, anym] + [vmem] * 4,
        out_specs=vmem,
        scratch_shapes=[V((n, domb + 1, npno, blk), BF)] * 4 + [
            V((n_occ + 8, req * per + 1, 8, blk), BF),
            V((n_occ, n * per + 1, 8, blk), BF),
            V((n_occ, n, 8, blk), BF),
            V((n_occ, n * (per - 1) + 1, 8, blk), BF),
            V((n_occ, req * per + 1, 8, blk), BF),
            V((rows, 128), F32),
            V((tiles // 2, 8, 128), BF),
            V((n_rep, tiles // 2, 8, 128), BF),
            V((n * tiles, 128), F32),
            V((rows, 128), F32),
            V((rows, 128), F32),
            V((rows, 128), F32),
            V((1, 128), i32),
            V((n_occ, 1, 128), i32),
            pltpu.SMEM((n_occ, 1, 128), i32),
            V((domains.shape[0], domb + -domb % 8), i32),
            V((2 * group + 2 * req, 128), i32),
            pltpu.SMEM((2 * group + 2 * req, 128), i32),
            pltpu.SMEM((2 * req * domb,), i32),
            V((n * npno, n * npno), F32),
            V((group // 2 + n, 128, 128), F32),
            V((2 * req + n, npno, 128), F32),
            V((rows, 128), F32),
            V((rows, 128), F32),
            V((rows, 128), F32),
            V((rows, 128), F32),
            V((rows, 128), F32),
            dma((6,)), dma((6,)), dma((n_rep,)), dma((n_rep,)),
            dma((3,)), dma((3,)), dma((2,)), dma((2,)), dma((2,)), dma((2,)), dma((4 + n * per,)),
        ],
        compiler_params=pltpu.CompilerParams(
            collective_id=0, has_side_effects=True, vmem_limit_bytes=56 * 1024 * 1024),
    )(pno_count, far_owner.T, far_pair.T, coeffs, coeffs.reshape(n, per, n_occ, 8, blk),
      amplitudes, denominators, near_pair, domains.T)


def solution(mesh):
    both = ("occ", "rep")
    in_specs = (
        P(both, None, None, None), P(both, None), P(both, None), P(both),
        P(), P(both, None), P(both, None), P(both, None),
    )
    return jax.shard_map(
        functools.partial(on_device, mesh.shape["occ"], mesh.shape["rep"]),
        mesh=mesh, in_specs=in_specs, out_specs=P(both, None), check_vma=False,
    )
```

```python
import functools

import jax
import jax.numpy as jnp
from jax import lax
from jax.experimental import pallas as pl
from jax.experimental.pallas import tpu as pltpu
from jax.sharding import PartitionSpec as P

MESH = pl.DeviceIdType.MESH
NBLK = 32
KN = 2
BF = jnp.bfloat16
F32 = jnp.float32
NT = (((1,), (1,)), ((), ()))


def split(x):
    hi = x.astype(BF)
    return hi, (x - hi.astype(F32)).astype(BF)


def mm(a, b):
    return jnp.dot(a, b, preferred_element_type=F32)


def mm_nt(a, b):
    return lax.dot_general(a, b, NT, preferred_element_type=F32)


def kernel(
    n_occ, n_rep, n, domb, npno, blk, nx, nz,
    cnt, fown, fpair, coef, coefs, amp, den, near, dom,
    out,
    G0, G1, G2, G3, F, PS, RA, RZ, SF, T0, TP, GP, GT, RT, ST, FT, RR, RQ, rqs, DT, IV, ivs, FI, acc, BD, SS, W,
    BKs, BKr, BS, BB, X,
    ysend, yrecv, tsend, trecv, p1s, p1r, p2s, p2r, bs, br, lsem,
):
    me = lax.axis_index("occ")
    rep = lax.axis_index("rep")
    cores = n_occ // (nx * nz)
    mx, mz, mc = me // (nz * cores), lax.rem(me // cores, nz), lax.rem(me, cores)
    req = n * KN
    group = n * n_rep
    tiles = npno * npno // 128
    per = domb * npno // 8 // n_occ
    lane = lax.broadcasted_iota(jnp.int32, (8, 128), 1)
    sub = lax.broadcasted_iota(jnp.int32, (8, 128), 0)
    low = lane < npno
    G = (G0, G1, G2, G3)

    def occ_dev(d):
        return {"occ": d}

    def rep_dev(r):
        return {"rep": lax.rem(rep + r, n_rep)}

    def at(dx, dz, dc):
        return (lax.rem(mx + dx, nx) * nz + lax.rem(mz + dz, nz)) * cores + lax.rem(mc + dc, cores)

    def span(d, m):
        return min(d, m - d)

    outward = sorted(
        [(dx, dz, dc) for dc in range(cores) for dz in range(nz) for dx in range(nx) if (dx, dz, dc) != (0, 0, 0)],
        key=lambda o: -(span(o[0], nx) + span(o[1], nz)))

    barrier = pltpu.get_barrier_semaphore()
    for o in outward:
        pl.semaphore_signal(barrier, inc=1, device_id=occ_dev(at(*o)), device_id_type=MESH)
    for r in range(1, n_rep):
        pl.semaphore_signal(barrier, inc=1, device_id=rep_dev(r), device_id_type=MESH)

    blocks = pl.ds(0, domb)
    own = pltpu.make_async_copy(coef, G0.at[:, blocks], lsem.at[0])
    own.start()
    cuts = [
        pltpu.make_async_copy(coefs.at[p, t], PS.at[:, n * t + p], lsem.at[4 + per * p + t])
        for p in range(n) for t in range(per)]
    for c in cuts:
        c.start()

    rr = jnp.zeros((1, 128), jnp.int32)
    lane1 = lax.broadcasted_iota(jnp.int32, (1, 128), 1)
    base = lax.rem(me * req, 128)
    for j in range(req):
        rr = jnp.where(lane1 == base + j, fown[j % KN, j // KN] * 8 + fpair[j % KN, j // KN], rr)
    RR[...] = rr
    RQ[me] = rr

    cntv = jnp.zeros((8, 128), jnp.int32)
    for p in range(n):
        cntv = jnp.where(sub == p, cnt[p], cntv)
    col = lax.rem(lane, npno)
    up = lane // npno
    pad = jnp.zeros((8 - n, 128), F32)
    last = None
    for i in range(tiles):
        x = jnp.concatenate([amp[:, 128 * i : 128 * i + 128].astype(F32), pad], axis=0)
        live = (2 * i + up < cntv) & (col < cntv)
        x = jnp.where(live, x, 0.0)
        T0[pl.ds(8 * i, 8), :] = x
        PS[i, n * per] = x.astype(BF)
        if i % 2:
            TP[i // 2] = (last + pltpu.roll(x, n, 0)).astype(BF)
        last = x

    dt = jnp.concatenate([dom[...], jnp.zeros((-domb % 8, dom.shape[1]), jnp.int32)], axis=0)
    DT[...] = dt.T
    rows_d = [DT[pl.ds(pl.multiple_of(me * group, group), group), :]]
    for j in range(req):
        owner, pair = fown[j % KN, j // KN], fpair[j % KN, j // KN]
        rows_d.append(DT[pl.ds((owner * n_rep + rep) * n + pair, 1), :])
    dd = jnp.concatenate(rows_d, axis=0)
    lane_i = lax.broadcasted_iota(jnp.int32, (group + req, 128), 1)
    inv = jnp.full((group + req, 128), domb, jnp.int32)
    for a in range(domb):
        inv = jnp.where(dd[:, a : a + 1] == lane_i, a, inv)
    IV[pl.ds(0, group), :] = inv[:group]
    fi = inv[group:]
    have = fi < domb
    IV[pl.ds(group, req), :] = jnp.where(have, lax.rem(fi * 8, n_occ), n_occ)
    IV[pl.ds(group + req, req), :] = jnp.where(have, (fi * 8) // n_occ, 0)
    IV[pl.ds(group + 2 * req, group), pl.ds(0, dd.shape[1])] = dd[:group]

    for g in G:
        g[:, domb] = jnp.zeros((n, npno, blk), BF)
    for j in range(req):
        F[pl.ds(n_occ, 8), j] = jnp.zeros((8, 8, blk), BF)
    for c in cuts:
        c.wait()
    RA[me] = PS[me, pl.ds(0, n)]
    RZ[me] = PS[me, pl.ds(n, n * (per - 1) + 1)]

    pl.semaphore_wait(barrier, n_occ - 1 + n_rep - 1)
    index = pltpu.make_async_copy(IV, ivs, lsem.at[3])
    index.start()

    half = n // 2
    ahead, behind = 1, n_rep - 1
    opposite = n_rep // 2

    def halfway(src, h, to, r, s):
        return pltpu.make_async_remote_copy(
            src, G[to].at[pl.ds(h * half, half), blocks], ysend.at[s], yrecv.at[s],
            device_id=rep_dev(r), device_id_type=MESH)

    firsts = [
        halfway(coef.at[pl.ds(0, half)], 0, behind, ahead, 0),
        halfway(coef.at[pl.ds(half, half)], 1, ahead, behind, 1),
        halfway(coef.at[pl.ds(half, half)], 1, behind, ahead, 2),
        halfway(coef.at[pl.ds(0, half)], 0, ahead, behind, 3)]
    relays = [
        halfway(G[behind].at[pl.ds(0, half), blocks], 0, opposite, ahead, 4),
        halfway(G[ahead].at[pl.ds(half, half), blocks], 1, opposite, behind, 5)]
    firsts[0].start()
    firsts[1].start()
    amps = []
    for r in range(1, n_rep):
        t = pltpu.make_async_remote_copy(
            TP, GP.at[n_rep - r], tsend.at[r], trecv.at[n_rep - r], device_id=rep_dev(r), device_id_type=MESH)
        t.start()
        amps.append(t)
    firsts[2].start()
    firsts[3].start()

    def slices(o, piece):
        d = at(*o)
        part, to = (pl.ds(n, n * (per - 1) + 1), RZ) if piece else (pl.ds(0, n), RA)
        pltpu.make_async_remote_copy(
            PS.at[d, part], to.at[me], p1s.at[1 + piece], p1r.at[1 + piece],
            device_id=occ_dev(d), device_id_type=MESH).start()

    for o in outward[:8]:
        slices(o, 0)
    for o in outward:
        pltpu.make_async_remote_copy(
            RR, RQ.at[me], p1s.at[0], p1r.at[0], device_id=occ_dev(at(*o)), device_id_type=MESH).start()
    for o in outward[8:]:
        slices(o, 0)
    for o in outward:
        slices(o, 1)

    def wait_all(ref, sem):
        pltpu.make_async_copy(ref, ref, sem).wait()

    index.wait()
    own.wait()
    GP[0] = TP[...]
    lane32 = lax.broadcasted_iota(jnp.int32, (npno // 2, 128), 1) < npno
    low64 = lax.broadcasted_iota(jnp.int32, (npno, 128), 1) < npno

    def place(x, slot, odd):
        other = pltpu.roll(x, npno, 1)
        if odd:
            BD[slot, pl.ds(npno, npno // 2, stride=2), :] = jnp.where(lane32, 0.0, other)
            BD[slot, pl.ds(npno + 1, npno // 2, stride=2), :] = jnp.where(lane32, 0.0, x)
        else:
            BD[slot, pl.ds(0, npno // 2, stride=2), :] = jnp.where(lane32, x, 0.0)
            BD[slot, pl.ds(1, npno // 2, stride=2), :] = jnp.where(lane32, other, 0.0)

    def near_part(r, gains):
        dev = lax.rem(rep + r, n_rep)
        acc[...] = jnp.zeros_like(acc)

        def overlap(b, c):
            hs, gs = [], []
            for t in range(4):
                bb = 4 * b + t
                hs.append(jnp.concatenate([G0[p, ivs[rep * n + p, bb]] for p in range(n)], axis=0))
                gs.append(jnp.concatenate([G[r][q, ivs[dev * n + q, bb]] for q in range(n)], axis=0))
            acc[...] += mm_nt(jnp.concatenate(hs, axis=1), jnp.concatenate(gs, axis=1))
            return c

        lax.fori_loop(0, NBLK // 4, overlap, 0)
        GT[...] = GP[r].astype(F32).reshape(n * tiles, 128)
        for q in range(n):
            place(GT[pl.ds(q, npno // 2, stride=n), :], (n * r + q) // 2, q % 2)
        parts = [[] for _ in range(n)]
        for k in range(n // 2):
            hi, lo = split(acc[:, 128 * k : 128 * k + 128])
            bd = BD[n // 2 * r + k].astype(BF)
            u = mm(jnp.concatenate([hi, lo], axis=1), jnp.concatenate([bd, bd], axis=0))
            q = dev * n + 2 * k
            c0 = jnp.sum((near[...] == q).astype(F32), axis=1, keepdims=True)
            c1 = jnp.sum((near[...] == q + 1).astype(F32), axis=1, keepdims=True)
            w = jnp.where(low[:n], c0, c1)
            for p in range(n):
                rows = slice(p * npno, (p + 1) * npno)
                uh, ul = split(u[rows] * w[p : p + 1])
                parts[p].append((uh, ul, hi[rows], lo[rows]))
        for p in range(n):
            uh, ul, sh, sl = (jnp.concatenate(v, axis=1) for v in zip(*parts[p]))
            g = mm_nt(uh, sh) + mm_nt(ul, sh) + mm_nt(uh, sl)
            if gains:
                g = g + W[2 * req + p, :, pl.ds(0, npno)]
            W[2 * req + p, :, pl.ds(0, npno)] = g

    near_part(0, False)

    wait_all(RQ.at[pl.ds(0, n_occ - 1)], p1r.at[0])
    table = pltpu.make_async_copy(RQ, rqs, lsem.at[2])
    table.start()
    table.wait()
    others = pl.ds(0, n_occ - 1)
    cut = (pl.ds(0, req), pl.ds(req, req * (per - 1) + 1))

    def gather(d, dst, piece):
        for j in range(req):
            r = rqs[d, 0, lax.rem(d * req + j, 128)]
            src, pair = r >> 3, r & 7
            if piece:
                for t in range(per - 1):
                    dst[d, req * (t + 1) + j] = RZ[src, n * t + pair]
                ST[pl.ds(8 * d + j, 1), :] = RT[pl.ds(r, 1), :]
            else:
                dst[d, j] = RA[src, pair]
        if piece:
            dst[d, req * per] = ST[pl.ds(8 * d, 8), :].astype(BF)

    def ship(d, piece):
        pltpu.make_async_remote_copy(
            SF.at[d, cut[piece]], F.at[me, cut[piece]], p2s.at[piece], p2r.at[piece],
            device_id=occ_dev(d), device_id_type=MESH).start()

    def answer_all(piece):
        last = None
        for o in outward:
            d = at(*o)
            gather(d, SF, piece)
            if last is not None:
                ship(last, piece)
            last = d
        ship(last, piece)

    wait_all(RA.at[others], p1r.at[1])
    answer_all(0)
    for t in range(2):
        firsts[t].wait_recv()
        relays[t].start()
    wait_all(RZ.at[others], p1r.at[2])
    RT[...] = RZ[:, n * (per - 1)].astype(F32).reshape(8 * n_occ, 128)
    answer_all(1)
    gather(me, F, 0)
    gather(me, F, 1)

    for t in amps:
        t.wait_recv()
    firsts[3].wait_recv()
    near_part(ahead, True)
    firsts[2].wait_recv()
    near_part(behind, True)

    for j in range(req):
        for a in range(domb):
            b = ivs[group + 2 * req + rep * n + j // KN, a]
            FI[2 * (j * domb + a)] = ivs[group + j, b]
            FI[2 * (j * domb + a) + 1] = req * ivs[group + req + j, b] + j
    for t in range(2):
        wait_all(F.at[others, cut[t]], p2r.at[t])
    def flat(slot):
        e = W[slot, pl.ds(0, npno // 2, stride=2), :]
        o = W[slot, pl.ds(1, npno // 2, stride=2), :]
        return jnp.where(lane32, e, pltpu.roll(o, npno, 1))

    def block(j, a):
        at_ja = 2 * (j * domb + a)
        return F[pl.ds(FI[at_ja], 8), FI[at_ja + 1]].reshape(npno, blk)

    z = jnp.zeros((npno, 128), BF)
    for p in range(n):
        h = jnp.concatenate([G0[p, a] for a in range(domb)], axis=1)
        f = jnp.concatenate([
            jnp.concatenate([block(j, a) for a in range(domb)], axis=1)
            for j in range(KN * p, KN * p + KN)], axis=0)
        s = mm_nt(h, f)
        sh, sl = split(s)
        th, tl = split(s.T)
        SS[p] = s
        odd = p % 2
        tp = BD[p // 2, pl.ds(odd * npno, npno), :].astype(BF)
        v = mm(jnp.concatenate([tp, tp], axis=1),
               jnp.concatenate([z, sh, z, sl] if odd else [sh, z, sl, z], axis=0))
        vh, vl = split(v)
        b = mm(th, vh) + mm(tl, vh) + mm(th, vl)
        W[KN * p, :, :] = b[:npno]
        W[KN * p + 1, :, :] = pltpu.roll(b[npno:], npno, 1)
    for j in range(req):
        BKs[pl.ds(j, npno // 2, stride=8), :] = flat(j)

    def back(src, dst, s):
        for o in outward:
            d = at(*o)
            pltpu.make_async_remote_copy(
                src.at[pl.ds(8 * d, 8)], dst.at[pl.ds(8 * me, 8)], bs.at[s], br.at[s],
                device_id=occ_dev(d), device_id_type=MESH).start()
        dst[pl.ds(8 * me, 8), :] = src[pl.ds(8 * me, 8), :]

    rows_in = pl.ds(0, 8 * (n_occ - 1))
    back(BKs, BKr, 0)
    FT[...] = F[pl.ds(0, n_occ), req * per].astype(F32).reshape(8 * n_occ, 128)
    for j in range(req):
        place(FT[pl.ds(j, npno // 2, stride=8), :], (group + j) // 2, j % 2)
    for p in range(n):
        sh, sl = split(SS[p])
        bd = BD[group // 2 + p].astype(BF)
        u = mm(jnp.concatenate([sh, sl], axis=1), jnp.concatenate([bd, bd], axis=0))
        uh, ul = split(u)
        W[2 * req + p, :, pl.ds(0, npno)] += mm_nt(uh, sh) + mm_nt(ul, sh) + mm_nt(uh, sl)
    for t in relays:
        t.wait_recv()
    near_part(opposite, True)
    hn = n_occ // 2
    ids = jnp.concatenate(
        [jnp.sum(RQ[pl.ds(h * hn, hn)], axis=0) for h in range(2)], axis=1)
    hot = (lax.broadcasted_iota(jnp.int32, (8 * n_occ, req * n_occ), 0) == ids).astype(F32).astype(BF)
    wait_all(BKr.at[rows_in], br.at[0])
    kh, kl = split(BKr[...])
    BS[...] = mm(hot, kh) + mm(hot, kl)
    back(BS, BB, 1)
    for p in range(n):
        X[pl.ds(p, npno // 2, stride=8), :] = flat(2 * req + p)
    de = jnp.concatenate([den[...], jnp.zeros((8 - n, npno), F32)], axis=0)
    db = jnp.concatenate([de, de], axis=1)
    for i in range(tiles):
        r = pl.ds(8 * i, 8)
        da = jnp.where(low, de[:, 2 * i : 2 * i + 1], de[:, 2 * i + 1 : 2 * i + 2])
        X[r, :] = (da + db) * T0[r, :] + X[r, :]
    wait_all(BB.at[rows_in], br.at[1])
    for i in range(tiles):
        r = pl.ds(8 * i, 8)
        live = (2 * i + up < cntv) & (col < cntv)
        out[:, 128 * i : 128 * i + 128] = jnp.where(live, X[r, :] + BB[r, :], 0.0)[:n]

    for c in firsts + relays + amps:
        c.wait_send()
    wait_all(RQ.at[pl.ds(0, n_occ - 1)], p1s.at[0])
    wait_all(RA.at[others], p1s.at[1])
    wait_all(RZ.at[others], p1s.at[2])
    for t in range(2):
        wait_all(F.at[others, cut[t]], p2s.at[t])
    wait_all(BKr.at[rows_in], bs.at[0])
    wait_all(BB.at[rows_in], bs.at[1])


def on_device(n_occ, n_rep, coeffs, amplitudes, denominators, pno_count, domains, far_owner, far_pair, near_pair):
    n, domb, npno, blk = coeffs.shape
    group = n * n_rep
    req = n * KN
    i32 = jnp.int32
    smem = pl.BlockSpec(memory_space=pltpu.SMEM)
    vmem = pl.BlockSpec(memory_space=pltpu.VMEM)
    anym = pl.BlockSpec(memory_space=pl.ANY)
    rows = 8 * n_occ
    per = domb * npno // 8 // n_occ
    tiles = npno * npno // 128
    V = pltpu.VMEM
    dma = pltpu.SemaphoreType.DMA
    return pl.pallas_call(
        functools.partial(kernel, n_occ, n_rep, n, domb, npno, blk, 4, 4),
        out_shape=jax.ShapeDtypeStruct((n, npno * npno), F32),
        in_specs=[smem] * 3 + [anym, anym] + [vmem] * 4,
        out_specs=vmem,
        scratch_shapes=[V((n, domb + 1, npno, blk), BF)] * 4 + [
            V((n_occ + 8, req * per + 1, 8, blk), BF),
            V((n_occ, n * per + 1, 8, blk), BF),
            V((n_occ, n, 8, blk), BF),
            V((n_occ, n * (per - 1) + 1, 8, blk), BF),
            V((n_occ, req * per + 1, 8, blk), BF),
            V((rows, 128), F32),
            V((tiles // 2, 8, 128), BF),
            V((n_rep, tiles // 2, 8, 128), BF),
            V((n * tiles, 128), F32),
            V((rows, 128), F32),
            V((rows, 128), F32),
            V((rows, 128), F32),
            V((1, 128), i32),
            V((n_occ, 1, 128), i32),
            pltpu.SMEM((n_occ, 1, 128), i32),
            V((domains.shape[0], domb + -domb % 8), i32),
            V((2 * group + 2 * req, 128), i32),
            pltpu.SMEM((2 * group + 2 * req, 128), i32),
            pltpu.SMEM((2 * req * domb,), i32),
            V((n * npno, n * npno), F32),
            V((group // 2 + n, 128, 128), F32),
            V((n, npno, KN * npno), F32),
            V((2 * req + n, npno, 128), F32),
            V((rows, 128), F32),
            V((rows, 128), F32),
            V((rows, 128), F32),
            V((rows, 128), F32),
            V((rows, 128), F32),
            dma((6,)), dma((6,)), dma((n_rep,)), dma((n_rep,)),
            dma((3,)), dma((3,)), dma((2,)), dma((2,)), dma((2,)), dma((2,)), dma((4 + n * per,)),
        ],
        compiler_params=pltpu.CompilerParams(
            collective_id=0, has_side_effects=True, vmem_limit_bytes=56 * 1024 * 1024),
    )(pno_count, far_owner.T, far_pair.T, coeffs, coeffs.reshape(n, per, n_occ, 8, blk),
      amplitudes, denominators, near_pair, domains.T)


def solution(mesh):
    both = ("occ", "rep")
    in_specs = (
        P(both, None, None, None), P(both, None), P(both, None), P(both),
        P(), P(both, None), P(both, None), P(both, None),
    )
    return jax.shard_map(
        functools.partial(on_device, mesh.shape["occ"], mesh.shape["rep"]),
        mesh=mesh, in_specs=in_specs, out_specs=P(both, None), check_vma=False,
    )
```
